32 devices in a mesh: win: 8 (over z, x), atom: 4 (over y, core).
Axes of the slice: x: 2, y: 2, z: 4, core: 2. Of those that a mesh axis runs over, the one named last changes fastest.
Arguments:
- retarded: bfloat16 [64, 8, 2, 128, 128], P(('win', 'atom')), may hold values from -0.375 to 0.375
- sigma_in: bfloat16 [64, 8, 2, 128, 128], P(('win', 'atom')), may hold values from -6 to 6
- bit_shifts: int32 [3], replicated, may hold values from 0 to 2, as said below
- occupation: float32 [3], replicated, may hold values from 0.3 to 3
- neighbors: int32 [8, 3], replicated, may hold values from 0 to 7, as said below
- coupling: bfloat16 [3, 128, 128], replicated, may hold values from -0.375 to 0.375
Outputs:
- self_energy: bfloat16 [64, 8, 2, 128, 128], P('win', 'atom')
The draws below stay inside these ranges and needn't reach their ends.
Inputs may be any that keep to these rules, and one draw needn't show every extreme that they name: `bit_shifts`: three different values; among them are 0 and 2, in an order drawn afresh. `neighbors`: column 0 of row b is b itself; the other columns of row b lie within b - 1 to b + 1.
All inputs are finite; a program needn't handle non-finite values.
Results may differ from the reference program's by a relative error of at most 0.007.
Values may be sent and summed in bfloat16 or wider, within the bound.
No kernel may reach another device: no remote copies, remote signals or barrier semaphores. Data moves between devices by JAX's collectives and lax.ppermute only.
A program may use at most 128 MiB of HBM per device.

```python
import math
import jax
import jax.numpy as jnp
from jax import lax

NORB = 128
MODES = 3
DIRS = 3
EW = 8
NE = 64
NB = 8
WBITS = 3
N_WIN = 8


def draw_bit_shifts(key, part):
    middle = jax.random.randint(key, (), 1, WBITS - 1).astype(jnp.int32)
    values = jnp.stack([jnp.int32(0), middle, jnp.int32(WBITS - 1)])
    order = jax.random.permutation(jax.random.fold_in(key, 7), 3)
    return values[order].astype(jnp.int32)


def draw_neighbors(key, part):
    offsets = jax.random.randint(key, (NB, DIRS - 1), -1, 2).astype(jnp.int32)
    blocks = jnp.arange(NB, dtype=jnp.int32)[:, None]
    others = jnp.clip(blocks + offsets, 0, NB - 1)
    return jnp.concatenate([blocks, others], axis=1).astype(jnp.int32)


def level_of(key, extent, cuts, smallest, largest):
    gain, own = 1.0, jax.random.fold_in(key, 6)
    for axis_at, blocks in cuts:
        heights = jnp.exp(jax.random.uniform(jax.random.fold_in(own, axis_at), (blocks,), jnp.float32, smallest / len(cuts), largest / len(cuts)))
        gain = gain * jnp.repeat(heights, extent[axis_at] // blocks).reshape([-1 if axis == axis_at else 1 for axis in range(len(extent))])
    return gain


def bell_draw(rng, dims, scale, most, cuts=(), kind=jnp.bfloat16):
    entries = jax.random.normal(rng, dims, jnp.float32) * scale
    if len(cuts) > 0:
        entries = level_of(rng, dims, cuts, -0.22, 0.18) * entries
    return jnp.clip(entries, min=-most, max=most).astype(kind)


def setup_inputs(seed: int = 0) -> dict:
    key_of = jax.random.split(jax.random.key(seed), 7)
    retarded = bell_draw(key_of[0], (NE, NB, 2, NORB, NORB), (2 * NORB) ** -0.5, 0.375, ((0, 32),))
    sigma_in = bell_draw(key_of[1], (NE, NB, 2, NORB, NORB), 1.0, 6.0, ((0, 32),))
    bit_shifts = draw_bit_shifts(jax.random.fold_in(key_of[6], 71), 0)
    occupation = jnp.clip(jnp.exp(jax.random.uniform(key_of[3], (MODES,), jnp.float32, math.log(0.3), math.log(3.0))), 0.3, 3.0)
    neighbors = draw_neighbors(jax.random.fold_in(key_of[6], 71), 0)
    coupling = bell_draw(key_of[5], (DIRS, NORB, NORB), (2 * NORB) ** -0.5, 0.375)
    return dict(retarded=retarded, sigma_in=sigma_in, bit_shifts=bit_shifts, occupation=occupation, neighbors=neighbors, coupling=coupling)


def complex_product(left, right, form):
    left = left.astype(jnp.float32)
    right = right.astype(jnp.float32)
    real_part = jnp.einsum(form, left[:, 0], right[:, 0]) - jnp.einsum(form, left[:, 1], right[:, 1])
    imag_part = jnp.einsum(form, left[:, 0], right[:, 1]) + jnp.einsum(form, left[:, 1], right[:, 0])
    return jnp.stack([real_part, imag_part], axis=1).astype(jnp.bfloat16)


def reference(retarded, sigma_in, bit_shifts, occupation, neighbors, coupling):
    def lesser_one(pair):
        green_one, sigma_one = pair
        product = complex_product(green_one, sigma_one, 'bij,bjk->bik')
        product = lax.optimization_barrier(product)
        return complex_product(product, green_one, 'bij,bkj->bik')

    lesser = lax.map(lesser_one, (retarded, sigma_in))
    windows = lesser.reshape(N_WIN, EW, NB, 2, NORB, NORB)
    coupling_f = coupling.astype(jnp.float32)

    def window_self(window):
        summed = jnp.zeros((EW, NB, 2, NORB, NORB), jnp.float32)
        for mode in range(MODES):
            partner = jnp.bitwise_xor(window, jnp.left_shift(jnp.int32(1), bit_shifts[mode]))
            summed = summed + occupation[mode] * windows[partner].astype(jnp.float32)
        partners = lax.optimization_barrier(summed.astype(jnp.bfloat16)).astype(jnp.float32)
        result = jnp.zeros((EW, NB, 2, NORB, NORB), jnp.float32)
        for direction in range(DIRS):
            picked = jnp.take(partners, neighbors[:, direction], axis=1)
            bent = jnp.einsum('ij,erxjk->erxik', coupling_f[direction], picked).astype(jnp.bfloat16)
            bent = lax.optimization_barrier(bent).astype(jnp.float32)
            result = result + jnp.einsum('erxij,kj->erxik', bent, coupling_f[direction])
        return result.astype(jnp.bfloat16)

    output = lax.map(window_self, jnp.arange(N_WIN, dtype=jnp.int32))
    return output.reshape(NE, NB, 2, NORB, NORB)
```

```python
import functools

import jax
import jax.numpy as jnp
from jax import lax
from jax.experimental import pallas as pl
from jax.experimental.pallas import tpu as pltpu
from jax.sharding import PartitionSpec as P


SMEM = pl.BlockSpec(memory_space=pltpu.SMEM)
VMEM = pl.BlockSpec(memory_space=pltpu.VMEM)
UNROLL = 8


def flip(value, axis, mask):
    pairs = [(source, source ^ mask) for source in range(lax.axis_size(axis))]
    return lax.ppermute(value, axis, pairs)


def contract(left, right, dims):
    return lax.dot_general(
        left, right, (dims, ((), ())), preferred_element_type=jnp.float32
    )


def over_blocks(count, step):
    chunk = UNROLL if count % UNROLL == 0 else 1
    if count == chunk:
        for block in range(count):
            step(block)
        return

    @pl.loop(0, count // chunk)
    def _(outer):
        for inner in range(chunk):
            step(outer * chunk + inner)


def lesser_of(real, imag, sigma_real, sigma_imag):
    left = jnp.concatenate([real, imag], axis=1)
    right = jnp.concatenate(
        [
            jnp.concatenate([sigma_real, sigma_imag], axis=1),
            jnp.concatenate([-sigma_imag, sigma_real], axis=1),
        ],
        axis=0,
    )
    product = contract(left, right, ((1,), (0,))).astype(jnp.bfloat16)
    flipped = jnp.concatenate(
        [
            jnp.concatenate([real, -imag], axis=1),
            jnp.concatenate([imag, real], axis=1),
        ],
        axis=0,
    )
    return contract(product, flipped, ((1,), (1,)))


def bend(coupling_ref, both, bent_ref, block):
    directions, size, _ = coupling_ref.shape
    stacked = coupling_ref[...].reshape(directions * size, size)
    bent = contract(stacked, both, ((1,), (0,))).astype(jnp.bfloat16)
    for direction in range(directions):
        rows = bent[direction * size : (direction + 1) * size]
        bent_ref[block, direction, 0] = rows[:, :size]
        bent_ref[block, direction, 1] = rows[:, size:]


def unbend(place, neighbors_ref, coupling_ref, bent_ref, out_refs):
    directions, size, _ = coupling_ref.shape
    wide = jnp.concatenate([coupling_ref[d] for d in range(directions)], axis=1)
    own = out_refs[0].shape[1]
    for distance, out_ref in enumerate(out_refs):
        for at in range(own):
            block = (place ^ distance) * own + at
            from_d = [neighbors_ref[block, d] for d in range(directions)]
            left = jnp.concatenate(
                [
                    jnp.concatenate(
                        [bent_ref[from_d[d], d, part] for d in range(directions)], axis=1
                    )
                    for part in range(2)
                ],
                axis=0,
            )
            total = contract(left, wide, ((1,), (1,))).astype(jnp.bfloat16)
            out_ref[0, at, 0] = total[:size]
            out_ref[0, at, 1] = total[size:]


def lesser_kernel(retarded_ref, sigma_ref, lesser_ref):
    size = retarded_ref.shape[-1]
    both = lesser_of(
        retarded_ref[0, 0, 0], retarded_ref[0, 0, 1], sigma_ref[0, 0, 0], sigma_ref[0, 0, 1]
    ).astype(jnp.bfloat16)
    lesser_ref[0, 0, 0] = both[:, :size]
    lesser_ref[0, 0, 1] = both[:, size:]


def lesser(retarded, sigma_in, first, count):
    _, blocks, parts, size, _ = retarded.shape
    spec = pl.BlockSpec((1, 1, parts, size, size), lambda e, b: (first + e, b, 0, 0, 0))
    return pl.pallas_call(
        lesser_kernel,
        out_shape=jax.ShapeDtypeStruct((count, blocks, parts, size, size), jnp.bfloat16),
        grid=(count, blocks),
        in_specs=[spec, spec],
        out_specs=pl.BlockSpec((1, 1, parts, size, size), lambda e, b: (e, b, 0, 0, 0)),
        cost_estimate=pl.CostEstimate(
            flops=count * blocks * 16 * size**3, bytes_accessed=count * blocks * 12 * size**2, transcendentals=0
        ),
        name="lesser",
    )(retarded, sigma_in)


def lesser_couple_kernel(
    place_ref, neighbors_ref, coupling_ref, retarded_ref, sigma_ref, *refs
):
    out_refs, bent_ref = refs[:-1], refs[-1]

    def one(block):
        both = lesser_of(
            retarded_ref[0, block, 0],
            retarded_ref[0, block, 1],
            sigma_ref[0, block, 0],
            sigma_ref[0, block, 1],
        ).astype(jnp.bfloat16)
        bend(coupling_ref, both, bent_ref, block)

    over_blocks(retarded_ref.shape[1], one)
    unbend(place_ref[0], neighbors_ref, coupling_ref, bent_ref, out_refs)


def sum_couple_kernel(
    taken, place_ref, bit_shifts_ref, occupation_ref, neighbors_ref, coupling_ref, *refs
):
    arrived, out_refs, bent_ref = refs[:taken], refs[taken:-1], refs[-1]
    weights = weights_of(taken, bit_shifts_ref, occupation_ref)

    def one(block):
        parts = []
        for part in range(2):
            total = weights[0] * arrived[0][0, block, part].astype(jnp.float32)
            for bit in range(1, taken):
                total += weights[bit] * arrived[bit][0, block, part].astype(jnp.float32)
            parts.append(total.astype(jnp.bfloat16))
        bend(coupling_ref, jnp.concatenate(parts, axis=1), bent_ref, block)

    over_blocks(arrived[0].shape[1], one)
    unbend(place_ref[0], neighbors_ref, coupling_ref, bent_ref, out_refs)


def weights_of(bits, bit_shifts_ref, occupation_ref):
    weights = []
    for bit in range(bits):
        weight = jnp.float32(0)
        for mode in range(bit_shifts_ref.shape[0]):
            weight += jnp.where(bit_shifts_ref[mode] == bit, occupation_ref[mode], 0.0)
        weights.append(weight)
    return weights


def coupled(kernel, scalars, coupling, arrays, first, count, atoms, name):
    _, blocks, parts, size, _ = arrays[0].shape
    directions = coupling.shape[0]
    own = blocks // atoms
    return pl.pallas_call(
        kernel,
        out_shape=[
            jax.ShapeDtypeStruct((count, own, parts, size, size), jnp.bfloat16)
            for _ in range(atoms)
        ],
        grid=(count,),
        in_specs=[SMEM] * len(scalars)
        + [VMEM]
        + [
            pl.BlockSpec((1, blocks, parts, size, size), lambda e: (first + e, 0, 0, 0, 0))
            for _ in arrays
        ],
        out_specs=[
            pl.BlockSpec((1, own, parts, size, size), lambda e: (e, 0, 0, 0, 0))
            for _ in range(atoms)
        ],
        scratch_shapes=[pltpu.VMEM((blocks, directions, parts, size, size), jnp.bfloat16)],
        cost_estimate=pl.CostEstimate(
            flops=count * blocks * directions * 8 * size**3,
            bytes_accessed=count * blocks * 12 * size**2,
            transcendentals=0,
        ),
        name=name,
    )(*scalars, coupling, *arrays)


def gather_kernel(distances, place_ref, *refs):
    pieces, out_ref, sem = refs[:distances], refs[distances], refs[distances + 1]
    count = pieces[0].shape[0]
    per = out_ref.shape[0] // distances
    copies = [
        pltpu.make_async_copy(
            pieces[distance], out_ref.at[pl.ds((place_ref[0] ^ distance) * per, count)], sem.at[distance]
        )
        for distance in range(distances)
    ]
    for copy in copies:
        copy.start()
    for copy in copies:
        copy.wait()


def place_first(place, pieces, energies):
    own = pieces[0].shape[1:]
    return pl.pallas_call(
        functools.partial(gather_kernel, len(pieces)),
        out_shape=jax.ShapeDtypeStruct((len(pieces) * energies, *own), jnp.bfloat16),
        in_specs=[SMEM] + [VMEM] * len(pieces),
        out_specs=pl.BlockSpec(memory_space=pl.ANY),
        scratch_shapes=[pltpu.SemaphoreType.DMA((len(pieces),))],
        name="place_first",
    )(place, *pieces)


def weighted_kernel(taken, place_ref, bit_shifts_ref, occupation_ref, *refs):
    arrived, out_ref = refs[:taken], refs[taken + 1]
    weights = weights_of(taken, bit_shifts_ref, occupation_ref)
    total = weights[0] * arrived[0][...].astype(jnp.float32)
    for bit in range(1, taken):
        total += weights[bit] * arrived[bit][...].astype(jnp.float32)
    out_ref[...] = total.astype(jnp.bfloat16).reshape(out_ref.shape)


def place_second(place, bit_shifts, occupation, arrived, out, energies, first):
    taken = len(arrived)
    distances, count, *own = arrived[0].shape
    spec = pl.BlockSpec((1, 1, *own), lambda d, e, *_: (d, e, 0, 0, 0, 0))
    return pl.pallas_call(
        functools.partial(weighted_kernel, taken),
        out_shape=jax.ShapeDtypeStruct(out.shape, out.dtype),
        grid_spec=pltpu.PrefetchScalarGridSpec(
            num_scalar_prefetch=3,
            grid=(distances, count),
            in_specs=[spec] * taken + [pl.BlockSpec(memory_space=pl.ANY)],
            out_specs=pl.BlockSpec(
                (1, *own),
                lambda d, e, place, *_: ((place[0] ^ d) * energies + first + e, 0, 0, 0, 0),
            ),
        ),
        input_output_aliases={3 + taken: 0},
        name="place_second",
    )(place, bit_shifts, occupation, *arrived, out)


def on_device(retarded, sigma_in, bit_shifts, occupation, neighbors, coupling):
    energies = retarded.shape[0]
    atoms = lax.axis_size("atom")
    bits = lax.axis_size("win").bit_length() - 1
    half = energies // 2
    rest = energies - half
    place = lax.axis_index("atom").astype(jnp.int32).reshape(1)

    lesser_a = lesser(retarded, sigma_in, 0, half)
    arrived_a = [flip(lesser_a, "win", 2**bit) for bit in reversed(range(bits))]

    coupled_b = coupled(
        lesser_couple_kernel, (place, neighbors), coupling, (retarded, sigma_in), half, rest, atoms, "lesser_couple"
    )
    exchanged_b = jnp.stack(
        [piece if d == 0 else flip(piece, "atom", d) for d, piece in enumerate(coupled_b)]
    )
    arrived_b = [flip(exchanged_b, "win", 2**bit) for bit in reversed(range(bits))]

    coupled_a = coupled(
        functools.partial(sum_couple_kernel, bits),
        (place, bit_shifts, occupation, neighbors),
        coupling,
        tuple(reversed(arrived_a)),
        0,
        half,
        atoms,
        "sum_couple",
    )
    exchanged_a = [piece if d == 0 else flip(piece, "atom", d) for d, piece in enumerate(coupled_a)]
    out = place_first(place, exchanged_a, energies)
    return place_second(place, bit_shifts, occupation, tuple(reversed(arrived_b)), out, energies, half)


def solution(mesh):
    return jax.shard_map(
        on_device,
        mesh=mesh,
        in_specs=(
            P(("win", "atom"), None, None, None, None),
            P(("win", "atom"), None, None, None, None),
            P(),
            P(),
            P(),
            P(),
        ),
        out_specs=P("win", "atom", None, None, None),
        check_vma=False,
    )
```

```python
import functools

import jax
import jax.numpy as jnp
from jax import lax
from jax.experimental import pallas as pl
from jax.experimental.pallas import tpu as pltpu
from jax.sharding import PartitionSpec as P


SMEM = pl.BlockSpec(memory_space=pltpu.SMEM)
VMEM = pl.BlockSpec(memory_space=pltpu.VMEM)
ANY = pl.BlockSpec(memory_space=pl.ANY)
UNROLL = 8
GROUP = 4
RESIDENT_BYTES = 1600 * 1024


def flip(value, axis, mask):
    pairs = [(source, source ^ mask) for source in range(lax.axis_size(axis))]
    return lax.ppermute(value, axis, pairs)


def contract(left, right, dims):
    return lax.dot_general(
        left, right, (dims, ((), ())), preferred_element_type=jnp.float32
    )


def over_blocks(count, step):
    chunk = UNROLL if count % UNROLL == 0 else 1
    if count == chunk:
        for block in range(count):
            step(block)
        return

    @pl.loop(0, count // chunk)
    def _(outer):
        for inner in range(chunk):
            step(outer * chunk + inner)


def lesser_of(real, imag, sigma_real, sigma_imag):
    left = jnp.concatenate([real, imag], axis=1)
    right = jnp.concatenate(
        [
            jnp.concatenate([sigma_real, sigma_imag], axis=1),
            jnp.concatenate([-sigma_imag, sigma_real], axis=1),
        ],
        axis=0,
    )
    product = contract(left, right, ((1,), (0,))).astype(jnp.bfloat16)
    flipped = jnp.concatenate(
        [
            jnp.concatenate([real, -imag], axis=1),
            jnp.concatenate([imag, real], axis=1),
        ],
        axis=0,
    )
    return contract(product, flipped, ((1,), (1,)))


def bend(coupling_ref, both, bent_ref, block):
    directions, size, _ = coupling_ref.shape
    stacked = coupling_ref[...].reshape(directions * size, size)
    bent = contract(stacked, both, ((1,), (0,))).astype(jnp.bfloat16)
    for direction in range(directions):
        rows = bent[direction * size : (direction + 1) * size]
        bent_ref[block, direction, 0] = rows[:, :size]
        bent_ref[block, direction, 1] = rows[:, size:]


def unbend(place, neighbors_ref, coupling_ref, bent_ref, out_refs):
    directions, size, _ = coupling_ref.shape
    wide = jnp.concatenate([coupling_ref[d] for d in range(directions)], axis=1)
    own = out_refs[0].shape[1]
    for distance, out_ref in enumerate(out_refs):
        for at in range(own):
            block = (place ^ distance) * own + at
            from_d = [neighbors_ref[block, d] for d in range(directions)]
            left = jnp.concatenate(
                [
                    jnp.concatenate(
                        [bent_ref[from_d[d], d, part] for d in range(directions)], axis=1
                    )
                    for part in range(2)
                ],
                axis=0,
            )
            total = contract(left, wide, ((1,), (1,))).astype(jnp.bfloat16)
            out_ref[0, at, 0] = total[:size]
            out_ref[0, at, 1] = total[size:]


def lesser_kernel(first, retarded_ref, sigma_ref, lesser_ref, green, sigma, result, sems):
    count, blocks, _, size, _ = lesser_ref.shape
    items = [(e, b) for e in range(count) for b in range(blocks)]
    loads = [
        (
            pltpu.make_async_copy(retarded_ref.at[first + e, b], green.at[i], sems.at[0, i]),
            pltpu.make_async_copy(sigma_ref.at[first + e, b], sigma.at[i], sems.at[1, i]),
        )
        for i, (e, b) in enumerate(items)
    ]
    for pair in loads:
        for copy in pair:
            copy.start()
    stores = []
    for start in range(0, len(items), GROUP):
        group = range(start, min(start + GROUP, len(items)))
        for i in group:
            for copy in loads[i]:
                copy.wait()
        for i in group:
            both = lesser_of(green[i, 0], green[i, 1], sigma[i, 0], sigma[i, 1])
            both = both.astype(jnp.bfloat16)
            result[i, 0] = both[:, :size]
            result[i, 1] = both[:, size:]
        for i in group:
            store = pltpu.make_async_copy(result.at[i], lesser_ref.at[items[i]], sems.at[2, i])
            store.start()
            stores.append(store)
    for store in stores:
        store.wait()


def lesser(retarded, sigma_in, first, count):
    _, blocks, parts, size, _ = retarded.shape
    slots = pltpu.VMEM((count * blocks, parts, size, size), jnp.bfloat16)
    return pl.pallas_call(
        functools.partial(lesser_kernel, first),
        out_shape=jax.ShapeDtypeStruct((count, blocks, parts, size, size), jnp.bfloat16),
        in_specs=[ANY, ANY],
        out_specs=ANY,
        scratch_shapes=[slots, slots, slots, pltpu.SemaphoreType.DMA((3, count * blocks))],
        cost_estimate=pl.CostEstimate(
            flops=count * blocks * 16 * size**3,
            bytes_accessed=count * blocks * 12 * size**2,
            transcendentals=0,
        ),
        name="lesser",
    )(retarded, sigma_in)


def lesser_couple_kernel(
    place_ref, neighbors_ref, coupling_ref, retarded_ref, sigma_ref, *refs
):
    out_refs, bent_ref = refs[:-1], refs[-1]

    def one(block):
        both = lesser_of(
            retarded_ref[0, block, 0],
            retarded_ref[0, block, 1],
            sigma_ref[0, block, 0],
            sigma_ref[0, block, 1],
        ).astype(jnp.bfloat16)
        bend(coupling_ref, both, bent_ref, block)

    over_blocks(retarded_ref.shape[1], one)
    unbend(place_ref[0], neighbors_ref, coupling_ref, bent_ref, out_refs)


def sum_couple_kernel(
    taken, place_ref, bit_shifts_ref, occupation_ref, neighbors_ref, coupling_ref, *refs
):
    arrived, out_refs, bent_ref = refs[:taken], refs[taken:-1], refs[-1]
    weights = weights_of(taken, bit_shifts_ref, occupation_ref)

    def one(block):
        parts = []
        for part in range(2):
            total = weights[0] * arrived[0][0, block, part].astype(jnp.float32)
            for bit in range(1, taken):
                total += weights[bit] * arrived[bit][0, block, part].astype(jnp.float32)
            parts.append(total.astype(jnp.bfloat16))
        bend(coupling_ref, jnp.concatenate(parts, axis=1), bent_ref, block)

    over_blocks(arrived[0].shape[1], one)
    unbend(place_ref[0], neighbors_ref, coupling_ref, bent_ref, out_refs)


def weights_of(bits, bit_shifts_ref, occupation_ref):
    weights = []
    for bit in range(bits):
        weight = jnp.float32(0)
        for mode in range(bit_shifts_ref.shape[0]):
            weight += jnp.where(bit_shifts_ref[mode] == bit, occupation_ref[mode], 0.0)
        weights.append(weight)
    return weights


def coupled(kernel, scalars, coupling, arrays, first, count, atoms):
    _, blocks, parts, size, _ = arrays[0].shape
    directions = coupling.shape[0]
    own = blocks // atoms
    return pl.pallas_call(
        kernel,
        out_shape=[
            jax.ShapeDtypeStruct((count, own, parts, size, size), jnp.bfloat16)
            for _ in range(atoms)
        ],
        grid=(count,),
        in_specs=[SMEM] * len(scalars)
        + [VMEM]
        + [
            pl.BlockSpec((1, blocks, parts, size, size), lambda e: (first + e, 0, 0, 0, 0))
            for _ in arrays
        ],
        out_specs=[
            pl.BlockSpec((1, own, parts, size, size), lambda e: (e, 0, 0, 0, 0))
            for _ in range(atoms)
        ],
        scratch_shapes=[pltpu.VMEM((blocks, directions, parts, size, size), jnp.bfloat16)],
        cost_estimate=pl.CostEstimate(
            flops=count * blocks * directions * 8 * size**3,
            bytes_accessed=count * blocks * 12 * size**2,
            transcendentals=0,
        ),
    )(*scalars, coupling, *arrays)


def gather_kernel(distances, place_ref, *refs):
    pieces, out_ref, sems = refs[:distances], refs[distances], refs[distances + 1]
    count = pieces[0].shape[0]
    per = out_ref.shape[0] // distances
    copies = []
    for distance, piece in enumerate(pieces):
        rows = pl.ds((place_ref[0] ^ distance) * per, count)
        copies.append(pltpu.make_async_copy(piece, out_ref.at[rows], sems.at[distance]))
        copies[-1].start()
    for copy in copies:
        copy.wait()


def in_vmem(arrays):
    if sum(array.size * array.dtype.itemsize for array in arrays) > RESIDENT_BYTES:
        return arrays
    return [pltpu.with_memory_space_constraint(array, pltpu.VMEM) for array in arrays]


def place_first(place, pieces, energies):
    own = pieces[0].shape[1:]
    return pl.pallas_call(
        functools.partial(gather_kernel, len(pieces)),
        out_shape=jax.ShapeDtypeStruct((len(pieces) * energies, *own), jnp.bfloat16),
        in_specs=[SMEM] + [VMEM] * len(pieces),
        out_specs=ANY,
        scratch_shapes=[pltpu.SemaphoreType.DMA((len(pieces),))],
        name="place_first",
    )(place, *in_vmem(pieces))


def weighted_kernel(
    taken, energies, first, place_ref, bit_shifts_ref, occupation_ref, *refs
):
    arrived, out_ref, result, sems = refs[:taken], *refs[taken + 1 :]
    weights = weights_of(taken, bit_shifts_ref, occupation_ref)
    distances, count = arrived[0].shape[:2]
    stores = []
    for d in range(distances):
        for e in range(count):
            total = weights[0] * arrived[0][d, e].astype(jnp.float32)
            for bit in range(1, taken):
                total += weights[bit] * arrived[bit][d, e].astype(jnp.float32)
            result[d, e] = total.astype(jnp.bfloat16)
            row = (place_ref[0] ^ d) * energies + first + e
            store = pltpu.make_async_copy(result.at[d, e], out_ref.at[row], sems.at[d, e])
            store.start()
            stores.append(store)
    for store in stores:
        store.wait()


def place_second(place, bit_shifts, occupation, arrived, out, energies, first):
    taken = len(arrived)
    return pl.pallas_call(
        functools.partial(weighted_kernel, taken, energies, first),
        out_shape=jax.ShapeDtypeStruct(out.shape, out.dtype),
        in_specs=[SMEM] * 3 + [VMEM] * taken + [ANY],
        out_specs=ANY,
        scratch_shapes=[
            pltpu.VMEM(arrived[0].shape, jnp.bfloat16),
            pltpu.SemaphoreType.DMA(arrived[0].shape[:2]),
        ],
        input_output_aliases={3 + taken: 0},
        name="place_second",
    )(place, bit_shifts, occupation, *in_vmem(arrived), out)


def on_device(retarded, sigma_in, bit_shifts, occupation, neighbors, coupling):
    energies = retarded.shape[0]
    atoms = lax.axis_size("atom")
    bits = lax.axis_size("win").bit_length() - 1
    half = energies // 2
    rest = energies - half
    place = lax.axis_index("atom").astype(jnp.int32).reshape(1)
    lesser_a = lesser(retarded, sigma_in, 0, half)
    arrived_a = {}
    for bit in reversed(range(bits)):
        arrived_a[bit] = flip(lesser_a, "win", 2**bit)

    coupled_b = coupled(
        lesser_couple_kernel, (place, neighbors), coupling, (retarded, sigma_in), half, rest, atoms
    )
    exchanged_b = [coupled_b[0]]
    for distance in range(1, atoms):
        exchanged_b.append(flip(coupled_b[distance], "atom", distance))
    exchanged_b = jnp.stack(exchanged_b)
    arrived_b = {}
    for bit in reversed(range(bits)):
        arrived_b[bit] = flip(exchanged_b, "win", 2**bit)

    coupled_a = coupled(
        functools.partial(sum_couple_kernel, bits),
        (place, bit_shifts, occupation, neighbors),
        coupling,
        tuple(arrived_a[bit] for bit in range(bits)),
        0,
        half,
        atoms,
    )
    exchanged_a = [coupled_a[0]]
    for distance in range(1, atoms):
        exchanged_a.append(flip(coupled_a[distance], "atom", distance))
    out = place_first(place, exchanged_a, energies)
    arrived_b = tuple(arrived_b[bit] for bit in range(bits))
    return place_second(place, bit_shifts, occupation, arrived_b, out, energies, half)


def solution(mesh):
    return jax.shard_map(
        on_device,
        mesh=mesh,
        in_specs=(
            P(("win", "atom"), None, None, None, None),
            P(("win", "atom"), None, None, None, None),
            P(),
            P(),
            P(),
            P(),
        ),
        out_specs=P("win", "atom", None, None, None),
        check_vma=False,
    )
```

```python
import functools
import math

import jax
import jax.numpy as jnp
from jax import lax
from jax.experimental import pallas as pl
from jax.experimental.pallas import tpu as pltpu
from jax.sharding import PartitionSpec as P


SMEM = pl.BlockSpec(memory_space=pltpu.SMEM)
VMEM = pl.BlockSpec(memory_space=pltpu.VMEM)
ANY = pl.BlockSpec(memory_space=pl.ANY)
UNROLL = 8
GROUP = 4
RESIDENT_BYTES = 1600 * 1024


def flip(value, axis, mask):
    pairs = [(source, source ^ mask) for source in range(lax.axis_size(axis))]
    return lax.ppermute(value, axis, pairs)


def contract(left, right, dims):
    return lax.dot_general(
        left, right, (dims, ((), ())), preferred_element_type=jnp.float32
    )


def over_blocks(count, step):
    chunk = math.gcd(count, UNROLL)
    if count == chunk:
        for block in range(count):
            step(block)
        return

    @pl.loop(0, count // chunk)
    def _(outer):
        for inner in range(chunk):
            step(outer * chunk + inner)


def kept(shape):
    if math.prod(shape) * 2 > RESIDENT_BYTES // 2:
        return jax.ShapeDtypeStruct(shape, jnp.bfloat16)
    return pltpu.VMEM(shape, jnp.bfloat16)


def in_vmem(arrays):
    if sum(array.size * array.dtype.itemsize for array in arrays) > RESIDENT_BYTES:
        return arrays
    return [pltpu.with_memory_space_constraint(array, pltpu.VMEM) for array in arrays]


def start_loads(first, count, blocks, retarded_ref, sigma_ref, green, sigma, sems):
    loads = []
    for i, (e, b) in enumerate((e, b) for e in range(count) for b in blocks):
        pair = (
            pltpu.make_async_copy(retarded_ref.at[first + e, b], green.at[i], sems.at[0, i]),
            pltpu.make_async_copy(sigma_ref.at[first + e, b], sigma.at[i], sems.at[1, i]),
        )
        for copy in pair:
            copy.start()
        loads.append(pair)
    return loads


def lesser_items(loads, green, sigma):
    for start in range(0, len(loads), GROUP):
        group = range(start, min(start + GROUP, len(loads)))
        for i in group:
            for copy in loads[i]:
                copy.wait()
        for i in group:
            both = lesser_of(green[i, 0], green[i, 1], sigma[i, 0], sigma[i, 1])
            yield i, both.astype(jnp.bfloat16)


def lesser_of(real, imag, sigma_real, sigma_imag):
    left = jnp.concatenate([real, imag], axis=1)
    right = jnp.concatenate(
        [
            jnp.concatenate([sigma_real, sigma_imag], axis=1),
            jnp.concatenate([-sigma_imag, sigma_real], axis=1),
        ],
        axis=0,
    )
    product = contract(left, right, ((1,), (0,))).astype(jnp.bfloat16)
    flipped = jnp.concatenate(
        [
            jnp.concatenate([real, -imag], axis=1),
            jnp.concatenate([imag, real], axis=1),
        ],
        axis=0,
    )
    return contract(product, flipped, ((1,), (1,)))


def bend(coupling_ref, both, bent_ref, block):
    directions, size, _ = coupling_ref.shape
    stacked = coupling_ref[...].reshape(directions * size, size)
    bent = contract(stacked, both, ((1,), (0,))).astype(jnp.bfloat16)
    for direction in range(directions):
        rows = bent[direction * size : (direction + 1) * size]
        bent_ref[block, direction, 0] = rows[:, :size]
        bent_ref[block, direction, 1] = rows[:, size:]


def unbend(place_ref, neighbors_ref, coupling_ref, bent_ref, out_refs, energy):
    directions, size, _ = coupling_ref.shape
    wide = jnp.concatenate([coupling_ref[d] for d in range(directions)], axis=1)
    own = out_refs[0].shape[1]
    for distance, out_ref in enumerate(out_refs):
        for at in range(own):
            block = (place_ref[0] ^ distance) * own + at
            from_d = [neighbors_ref[block, d] for d in range(directions)]
            left = jnp.concatenate(
                [
                    jnp.concatenate(
                        [bent_ref[from_d[d], d, part] for d in range(directions)], axis=1
                    )
                    for part in range(2)
                ],
                axis=0,
            )
            total = contract(left, wide, ((1,), (1,))).astype(jnp.bfloat16)
            out_ref[energy, at, 0] = total[:size]
            out_ref[energy, at, 1] = total[size:]


def lesser_kernel(first, cut, retarded_ref, sigma_ref, lesser_ref, green, sigma, sems):
    count, blocks, _, size, _ = lesser_ref.shape
    loads = start_loads(
        first, count, range(cut, cut + blocks), retarded_ref, sigma_ref, green, sigma, sems
    )
    for i, both in lesser_items(loads, green, sigma):
        for part in range(2):
            lesser_ref[i // blocks, i % blocks, part] = both[:, part * size : (part + 1) * size]


def lesser_rest_kernel(first, *refs):
    retarded_ref, sigma_ref, begun_ref, rest_ref, whole_ref, green, sigma, sems = refs
    count, blocks, _, size, _ = rest_ref.shape
    cut = begun_ref.shape[1]
    loads = start_loads(
        first, count, range(cut, cut + blocks), retarded_ref, sigma_ref, green, sigma, sems
    )
    whole_ref[:, :cut] = begun_ref[...]
    for i, both in lesser_items(loads, green, sigma):
        for part in range(2):
            half = both[:, part * size : (part + 1) * size]
            rest_ref[i // blocks, i % blocks, part] = half
            whole_ref[i // blocks, cut + i % blocks, part] = half


def lesser_scratch(count, blocks, own):
    slots = pltpu.VMEM((count * blocks, *own), jnp.bfloat16)
    return [slots, slots, pltpu.SemaphoreType.DMA((2, count * blocks))]


def lesser_cost(count, blocks, size):
    return pl.CostEstimate(
        flops=count * blocks * 16 * size**3,
        bytes_accessed=count * blocks * 12 * size**2,
        transcendentals=0,
    )


def lesser_begin(retarded, sigma_in, first, count, cut):
    own = retarded.shape[2:]
    return pl.pallas_call(
        functools.partial(lesser_kernel, first, 0),
        out_shape=kept((count, cut, *own)),
        in_specs=[ANY, ANY],
        out_specs=VMEM,
        scratch_shapes=lesser_scratch(count, cut, own),
        cost_estimate=lesser_cost(count, cut, own[-1]),
        name="lesser_begin",
    )(retarded, sigma_in)


def lesser_rest(retarded, sigma_in, begun, first, count):
    blocks, *own = retarded.shape[1:]
    rest = blocks - begun.shape[1]
    return pl.pallas_call(
        functools.partial(lesser_rest_kernel, first),
        out_shape=[kept((count, rest, *own)), kept((count, blocks, *own))],
        in_specs=[ANY, ANY, VMEM],
        out_specs=[VMEM, VMEM],
        scratch_shapes=lesser_scratch(count, rest, own),
        cost_estimate=lesser_cost(count, rest, own[-1]),
        name="lesser_rest",
    )(retarded, sigma_in, *in_vmem([begun]))


def lesser_couple_kernel(first, place_ref, neighbors_ref, coupling_ref, *refs):
    retarded_ref, sigma_ref, *out_refs, bent_ref, green, sigma, sems = refs
    blocks = retarded_ref.shape[1]
    count = out_refs[0].shape[0]
    loads = start_loads(
        first, count, range(blocks), retarded_ref, sigma_ref, green, sigma, sems
    )
    for i, both in lesser_items(loads, green, sigma):
        bend(coupling_ref, both, bent_ref, i % blocks)
        if i % blocks == blocks - 1:
            unbend(place_ref, neighbors_ref, coupling_ref, bent_ref, out_refs, i // blocks)


def lesser_couple(place, neighbors, coupling, retarded, sigma_in, first, count, atoms):
    blocks, *own = retarded.shape[1:]
    directions, size, _ = coupling.shape
    return pl.pallas_call(
        functools.partial(lesser_couple_kernel, first),
        out_shape=[kept((count, blocks // atoms, *own))] * atoms,
        in_specs=[SMEM, SMEM, VMEM, ANY, ANY],
        out_specs=[VMEM] * atoms,
        scratch_shapes=[pltpu.VMEM((blocks, directions, *own), jnp.bfloat16)]
        + lesser_scratch(count, blocks, own),
        cost_estimate=pl.CostEstimate(
            flops=count * blocks * (16 + directions * 8) * size**3,
            bytes_accessed=count * blocks * 12 * size**2,
            transcendentals=0,
        ),
        name="lesser_couple",
    )(place, neighbors, coupling, retarded, sigma_in)


def sum_couple_kernel(
    widths, place_ref, bit_shifts_ref, occupation_ref, neighbors_ref, coupling_ref, *refs
):
    taken = sum(widths)
    arrived, out_refs, bent_ref = list(refs[:taken]), refs[taken:-1], refs[-1]
    terms = [[arrived.pop(0) for _ in range(width)] for width in widths]
    weights = weights_of(len(terms), place_ref, bit_shifts_ref, occupation_ref)
    span = bent_ref.shape[0] // max(widths)
    for piece in range(max(widths)):

        def one(at, piece=piece):
            parts = []
            for part in range(2):
                total = None
                for weight, term in zip(weights, terms):
                    block = at if len(term) > 1 else piece * span + at
                    value = term[piece % len(term)][0, block, part].astype(jnp.float32)
                    total = weight * value if total is None else total + weight * value
                parts.append(total.astype(jnp.bfloat16))
            bend(coupling_ref, jnp.concatenate(parts, axis=1), bent_ref, piece * span + at)

        over_blocks(span, one)
    unbend(place_ref, neighbors_ref, coupling_ref, bent_ref, out_refs, 0)


def sum_couple(scalars, coupling, terms, atoms):
    count, blocks, *own = terms[0][0].shape
    directions = coupling.shape[0]
    arrays = [array for term in terms for array in term]
    return pl.pallas_call(
        functools.partial(sum_couple_kernel, [len(term) for term in terms]),
        out_shape=[
            jax.ShapeDtypeStruct((count, blocks // atoms, *own), jnp.bfloat16)
            for _ in range(atoms)
        ],
        grid=(count,),
        in_specs=[SMEM] * len(scalars)
        + [VMEM]
        + [pl.BlockSpec((1, *array.shape[1:]), lambda e: (e, 0, 0, 0, 0)) for array in arrays],
        out_specs=[
            pl.BlockSpec((1, blocks // atoms, *own), lambda e: (e, 0, 0, 0, 0))
            for _ in range(atoms)
        ],
        scratch_shapes=[pltpu.VMEM((blocks, directions, *own), jnp.bfloat16)],
        cost_estimate=pl.CostEstimate(
            flops=count * blocks * directions * 8 * own[-1] ** 3,
            bytes_accessed=count * blocks * 12 * own[-1] ** 2,
            transcendentals=0,
        ),
        name="sum_couple",
    )(*scalars, coupling, *arrays)


def weights_of(bits, place_ref, bit_shifts_ref, occupation_ref):
    weights = []
    for bit in range(bits):
        weight = jnp.float32(0)
        for mode in range(bit_shifts_ref.shape[0]):
            weight += jnp.where(bit_shifts_ref[mode] == bit, occupation_ref[mode], 0.0)
        weights.append(weight)
    if bits > 1:
        odd = place_ref[1] == 1
        low, high = weights[-2:]
        weights[-2:] = [jnp.where(odd, low, high), jnp.where(odd, high, low)]
    return weights


def gather_kernel(distances, place_ref, *refs):
    pieces, out_ref, sems = refs[:distances], refs[distances], refs[distances + 1]
    count = pieces[0].shape[0]
    per = out_ref.shape[0] // distances
    copies = []
    for distance, piece in enumerate(pieces):
        rows = pl.ds((place_ref[0] ^ distance) * per, count)
        copies.append(pltpu.make_async_copy(piece, out_ref.at[rows], sems.at[distance]))
        copies[-1].start()
    for copy in copies:
        copy.wait()


def place_first(place, pieces, energies):
    own = pieces[0].shape[1:]
    return pl.pallas_call(
        functools.partial(gather_kernel, len(pieces)),
        out_shape=jax.ShapeDtypeStruct((len(pieces) * energies, *own), jnp.bfloat16),
        in_specs=[SMEM] + [VMEM] * len(pieces),
        out_specs=ANY,
        scratch_shapes=[pltpu.SemaphoreType.DMA((len(pieces),))],
        name="place_first",
    )(place, *in_vmem(pieces))


def weighted_kernel(
    taken, energies, first, place_ref, bit_shifts_ref, occupation_ref, *refs
):
    arrived, out_ref, result, sems = refs[:taken], *refs[taken + 1 :]
    weights = weights_of(taken, place_ref, bit_shifts_ref, occupation_ref)
    distances, count = arrived[0].shape[:2]
    stores = []
    for d in range(distances):
        for e in range(count):
            total = weights[0] * arrived[0][d, e].astype(jnp.float32)
            for bit in range(1, taken):
                total += weights[bit] * arrived[bit][d, e].astype(jnp.float32)
            result[d, e] = total.astype(jnp.bfloat16)
            row = (place_ref[0] ^ d) * energies + first + e
            store = pltpu.make_async_copy(result.at[d, e], out_ref.at[row], sems.at[d, e])
            store.start()
            stores.append(store)
    for store in stores:
        store.wait()


def place_second(place, bit_shifts, occupation, arrived, out, energies, first):
    taken = len(arrived)
    return pl.pallas_call(
        functools.partial(weighted_kernel, taken, energies, first),
        out_shape=jax.ShapeDtypeStruct(out.shape, out.dtype),
        in_specs=[SMEM] * 3 + [VMEM] * taken + [ANY],
        out_specs=ANY,
        scratch_shapes=[
            pltpu.VMEM(arrived[0].shape, jnp.bfloat16),
            pltpu.SemaphoreType.DMA(arrived[0].shape[:2]),
        ],
        input_output_aliases={3 + taken: 0},
        name="place_second",
    )(place, bit_shifts, occupation, *in_vmem(arrived), out)


def stack_kernel(distances, *refs):
    pieces, out_ref, sems = refs[:distances], refs[distances], refs[distances + 1]
    copies = []
    for distance, piece in enumerate(pieces):
        copies.append(pltpu.make_async_copy(piece, out_ref.at[distance], sems.at[distance]))
        copies[-1].start()
    for copy in copies:
        copy.wait()


def stack(pieces):
    return pl.pallas_call(
        functools.partial(stack_kernel, len(pieces)),
        out_shape=jax.ShapeDtypeStruct((len(pieces), *pieces[0].shape), jnp.bfloat16),
        in_specs=[VMEM] * len(pieces),
        out_specs=ANY,
        scratch_shapes=[pltpu.SemaphoreType.DMA((len(pieces),))],
        name="stack",
    )(*in_vmem(pieces))


def term_masks(count):
    bits = count.bit_length() - 1
    masks = [(2**bit, 2**bit) for bit in range(bits)]
    if bits > 1:
        low, high = 2 ** (bits - 2), 2 ** (bits - 1)
        masks[-2:] = [(low, high), (high, low)]
    return masks


def oddness(window, count):
    bits = count.bit_length() - 1
    return (window >> (bits - 1) ^ window >> (bits - 2)) & 1 if bits > 1 else window & 0


def exchange(value, term):
    count = lax.axis_size("win")
    masks = term_masks(count)[term]
    pairs = [(source, source ^ masks[oddness(source, count)]) for source in range(count)]
    return lax.ppermute(value, "win", pairs)


def on_device(retarded, sigma_in, bit_shifts, occupation, neighbors, coupling):
    energies, blocks = retarded.shape[:2]
    atoms = lax.axis_size("atom")
    windows = lax.axis_size("win")
    terms = len(term_masks(windows))
    half = energies // 2
    rest = energies - half
    cut = blocks // 2
    place = jnp.stack(
        [lax.axis_index("atom"), oddness(lax.axis_index("win"), windows)]
    ).astype(jnp.int32)
    begun = lesser_begin(retarded, sigma_in, 0, half, cut)
    arrived_begun = exchange(begun, terms - 2)
    ended, lesser_a = lesser_rest(retarded, sigma_in, begun, 0, half)
    arrived_ended = exchange(ended, terms - 2)
    arrived_a = {}
    for term in reversed(range(terms)):
        if term != terms - 2:
            arrived_a[term] = [exchange(lesser_a, term)]
    arrived_a[terms - 2] = [arrived_begun, arrived_ended]

    coupled_b = lesser_couple(place, neighbors, coupling, retarded, sigma_in, half, rest, atoms)
    exchanged_b = [coupled_b[0]]
    for distance in range(1, atoms):
        exchanged_b.append(flip(coupled_b[distance], "atom", distance))
    exchanged_b = stack(exchanged_b)
    arrived_b = {}
    for term in range(terms):
        arrived_b[term] = exchange(exchanged_b, term)

    coupled_a = sum_couple(
        (place, bit_shifts, occupation, neighbors),
        coupling,
        [arrived_a[term] for term in range(terms)],
        atoms,
    )
    exchanged_a = [coupled_a[0]]
    for distance in range(1, atoms):
        exchanged_a.append(flip(coupled_a[distance], "atom", distance))
    out = place_first(place, exchanged_a, energies)
    arrived_b = tuple(arrived_b[term] for term in range(terms))
    return place_second(place, bit_shifts, occupation, arrived_b, out, energies, half)


def solution(mesh):
    return jax.shard_map(
        on_device,
        mesh=mesh,
        in_specs=(
            P(("win", "atom"), None, None, None, None),
            P(("win", "atom"), None, None, None, None),
            P(),
            P(),
            P(),
            P(),
        ),
        out_specs=P("win", "atom", None, None, None),
        check_vma=False,
    )
```

```python
import functools
import math

import jax
import jax.numpy as jnp
from jax import lax
from jax.experimental import pallas as pl
from jax.experimental.pallas import tpu as pltpu
from jax.sharding import PartitionSpec as P


SMEM = pl.BlockSpec(memory_space=pltpu.SMEM)
VMEM = pl.BlockSpec(memory_space=pltpu.VMEM)
ANY = pl.BlockSpec(memory_space=pl.ANY)
UNROLL = 8
GROUP = 4
RESIDENT_BYTES = 1600 * 1024


def flip(value, axis, mask):
    pairs = [(source, source ^ mask) for source in range(lax.axis_size(axis))]
    return lax.ppermute(value, axis, pairs)


def contract(left, right, dims):
    return lax.dot_general(
        left, right, (dims, ((), ())), preferred_element_type=jnp.float32
    )


def over_blocks(count, step):
    chunk = math.gcd(count, UNROLL)
    if count == chunk:
        for block in range(count):
            step(block)
        return

    @pl.loop(0, count // chunk)
    def _(outer):
        for inner in range(chunk):
            step(outer * chunk + inner)


def kept(shape):
    if math.prod(shape) * 2 > RESIDENT_BYTES // 2:
        return jax.ShapeDtypeStruct(shape, jnp.bfloat16)
    return pltpu.VMEM(shape, jnp.bfloat16)


def in_vmem(arrays):
    if sum(array.size * array.dtype.itemsize for array in arrays) > RESIDENT_BYTES:
        return arrays
    return [pltpu.with_memory_space_constraint(array, pltpu.VMEM) for array in arrays]


def start_loads(first, count, blocks, retarded_ref, sigma_ref, green, sigma, sems):
    loads = []
    for i, (e, b) in enumerate((e, b) for e in range(count) for b in blocks):
        pair = (
            pltpu.make_async_copy(retarded_ref.at[first + e, b], green.at[i], sems.at[0, i]),
            pltpu.make_async_copy(sigma_ref.at[first + e, b], sigma.at[i], sems.at[1, i]),
        )
        for copy in pair:
            copy.start()
        loads.append(pair)
    return loads


def lesser_items(loads, green, sigma, items):
    for i in items:
        for copy in loads[i]:
            copy.wait()
    for i in items:
        both = lesser_of(green[i, 0], green[i, 1], sigma[i, 0], sigma[i, 1])
        yield i, both.astype(jnp.bfloat16)


def lesser_of(real, imag, sigma_real, sigma_imag):
    left = jnp.concatenate([real, imag], axis=1)
    right = jnp.concatenate(
        [
            jnp.concatenate([sigma_real, sigma_imag], axis=1),
            jnp.concatenate([-sigma_imag, sigma_real], axis=1),
        ],
        axis=0,
    )
    product = contract(left, right, ((1,), (0,))).astype(jnp.bfloat16)
    flipped = jnp.concatenate(
        [
            jnp.concatenate([real, -imag], axis=1),
            jnp.concatenate([imag, real], axis=1),
        ],
        axis=0,
    )
    return contract(product, flipped, ((1,), (1,)))


def bend(coupling_ref, both, bent_ref, block):
    directions, size, _ = coupling_ref.shape
    stacked = coupling_ref[...].reshape(directions * size, size)
    bent = contract(stacked, both, ((1,), (0,))).astype(jnp.bfloat16)
    for direction in range(directions):
        rows = bent[direction * size : (direction + 1) * size]
        bent_ref[block, direction, 0] = rows[:, :size]
        bent_ref[block, direction, 1] = rows[:, size:]


def unbend(place_ref, neighbors_ref, coupling_ref, bent_ref, out_refs, energy):
    directions, size, _ = coupling_ref.shape
    wide = jnp.concatenate([coupling_ref[d] for d in range(directions)], axis=1)
    own = out_refs[0].shape[1]
    for distance, out_ref in enumerate(out_refs):
        for at in range(own):
            block = (place_ref[0] ^ distance) * own + at
            source = [neighbors_ref[d, block] for d in range(directions)]
            left = jnp.concatenate(
                [
                    jnp.concatenate(
                        [bent_ref[source[d], d, part] for d in range(directions)], axis=1
                    )
                    for part in range(2)
                ],
                axis=0,
            )
            total = contract(left, wide, ((1,), (1,))).astype(jnp.bfloat16)
            out_ref[energy, at, 0] = total[:size]
            out_ref[energy, at, 1] = total[size:]


def lesser_kernel(first, cut, retarded_ref, sigma_ref, lesser_ref, green, sigma, sems):
    count, blocks, _, size, _ = lesser_ref.shape
    loads = start_loads(
        first, count, range(cut, cut + blocks), retarded_ref, sigma_ref, green, sigma, sems
    )
    for i, both in lesser_items(loads, green, sigma, range(len(loads))):
        for part in range(2):
            lesser_ref[i // blocks, i % blocks, part] = both[:, part * size : (part + 1) * size]


def lesser_rest_kernel(first, *refs):
    retarded_ref, sigma_ref, begun_ref, rest_ref, whole_ref, green, sigma, sems = refs
    count, blocks, _, size, _ = rest_ref.shape
    cut = begun_ref.shape[1]
    loads = start_loads(
        first, count, range(cut, cut + blocks), retarded_ref, sigma_ref, green, sigma, sems
    )
    whole_ref[:, :cut] = begun_ref[...]
    for i, both in lesser_items(loads, green, sigma, range(len(loads))):
        for part in range(2):
            half = both[:, part * size : (part + 1) * size]
            rest_ref[i // blocks, i % blocks, part] = half
            whole_ref[i // blocks, cut + i % blocks, part] = half


def lesser_scratch(count, blocks, own):
    slots = pltpu.VMEM((count * blocks, *own), jnp.bfloat16)
    return [slots, slots, pltpu.SemaphoreType.DMA((2, count * blocks))]


def lesser_cost(count, blocks, size):
    return pl.CostEstimate(
        flops=count * blocks * 16 * size**3,
        bytes_accessed=count * blocks * 12 * size**2,
        transcendentals=0,
    )


def lesser_begin(retarded, sigma_in, first, count, cut):
    own = retarded.shape[2:]
    return pl.pallas_call(
        functools.partial(lesser_kernel, first, 0),
        out_shape=kept((count, cut, *own)),
        in_specs=[ANY, ANY],
        out_specs=VMEM,
        scratch_shapes=lesser_scratch(count, cut, own),
        cost_estimate=lesser_cost(count, cut, own[-1]),
        name="lesser_begin",
    )(retarded, sigma_in)


def lesser_rest(retarded, sigma_in, begun, first, count):
    blocks, *own = retarded.shape[1:]
    rest = blocks - begun.shape[1]
    return pl.pallas_call(
        functools.partial(lesser_rest_kernel, first),
        out_shape=[kept((count, rest, *own)), kept((count, blocks, *own))],
        in_specs=[ANY, ANY, VMEM],
        out_specs=[VMEM, VMEM],
        scratch_shapes=lesser_scratch(count, rest, own),
        cost_estimate=lesser_cost(count, rest, own[-1]),
        name="lesser_rest",
    )(retarded, sigma_in, *in_vmem([begun]))


def lesser_couple_kernel(first, place_ref, neighbors_ref, coupling_ref, *refs):
    retarded_ref, sigma_ref, *out_refs, bent_ref, made, green, sigma, sems = refs
    blocks = retarded_ref.shape[1]
    count = out_refs[0].shape[0]
    loads = start_loads(
        first, count, range(blocks), retarded_ref, sigma_ref, green, sigma, sems
    )
    for start in range(0, len(loads), GROUP):
        group = range(start, min(start + GROUP, len(loads)))
        for i, both in lesser_items(loads, green, sigma, group):
            made[i % GROUP] = both
        for i in group:
            bend(coupling_ref, made[i % GROUP], bent_ref, i % blocks)
            if i % blocks == blocks - 1:
                unbend(place_ref, neighbors_ref, coupling_ref, bent_ref, out_refs, i // blocks)


def lesser_couple(place, neighbors, coupling, retarded, sigma_in, first, count, atoms):
    blocks, *own = retarded.shape[1:]
    directions, size, _ = coupling.shape
    return pl.pallas_call(
        functools.partial(lesser_couple_kernel, first),
        out_shape=[kept((count, blocks // atoms, *own))] * atoms,
        in_specs=[SMEM, SMEM, VMEM, ANY, ANY],
        out_specs=[VMEM] * atoms,
        scratch_shapes=[
            pltpu.VMEM((blocks, directions, *own), jnp.bfloat16),
            pltpu.VMEM((GROUP, size, own[0] * size), jnp.bfloat16),
        ]
        + lesser_scratch(count, blocks, own),
        cost_estimate=pl.CostEstimate(
            flops=count * blocks * (16 + directions * 8) * size**3,
            bytes_accessed=count * blocks * 12 * size**2,
            transcendentals=0,
        ),
        name="lesser_couple",
    )(place, neighbors, coupling, retarded, sigma_in)


def sum_couple_kernel(
    widths, place_ref, odd_ref, bit_shifts_ref, occupation_ref, neighbors_ref, coupling_ref, *refs
):
    taken = sum(widths)
    arrived, out_refs, bent_ref = list(refs[:taken]), refs[taken:-1], refs[-1]
    terms = [[arrived.pop(0) for _ in range(width)] for width in widths]
    weights = weights_of(len(terms), odd_ref, bit_shifts_ref, occupation_ref)
    span = bent_ref.shape[0] // max(widths)
    for piece in range(max(widths)):

        def one(at, piece=piece):
            parts = []
            for part in range(2):
                total = None
                for weight, term in zip(weights, terms):
                    block = at if len(term) > 1 else piece * span + at
                    value = term[piece % len(term)][0, block, part].astype(jnp.float32)
                    total = weight * value if total is None else total + weight * value
                parts.append(total.astype(jnp.bfloat16))
            bend(coupling_ref, jnp.concatenate(parts, axis=1), bent_ref, piece * span + at)

        over_blocks(span, one)
    unbend(place_ref, neighbors_ref, coupling_ref, bent_ref, out_refs, 0)


def sum_couple(scalars, coupling, terms, atoms):
    count, blocks, *own = terms[0][0].shape
    directions = coupling.shape[0]
    arrays = [array for term in terms for array in term]
    return pl.pallas_call(
        functools.partial(sum_couple_kernel, [len(term) for term in terms]),
        out_shape=[
            jax.ShapeDtypeStruct((count, blocks // atoms, *own), jnp.bfloat16)
            for _ in range(atoms)
        ],
        grid=(count,),
        in_specs=[SMEM] * len(scalars)
        + [VMEM]
        + [pl.BlockSpec((1, *array.shape[1:]), lambda e: (e, 0, 0, 0, 0)) for array in arrays],
        out_specs=[
            pl.BlockSpec((1, blocks // atoms, *own), lambda e: (e, 0, 0, 0, 0))
            for _ in range(atoms)
        ],
        scratch_shapes=[pltpu.VMEM((blocks, directions, *own), jnp.bfloat16)],
        cost_estimate=pl.CostEstimate(
            flops=count * blocks * directions * 8 * own[-1] ** 3,
            bytes_accessed=count * blocks * 12 * own[-1] ** 2,
            transcendentals=0,
        ),
        name="sum_couple",
    )(*scalars, coupling, *arrays)


def weights_of(bits, odd_ref, bit_shifts_ref, occupation_ref):
    weights = []
    for bit in range(bits):
        weight = jnp.float32(0)
        for mode in range(bit_shifts_ref.shape[0]):
            weight += jnp.where(bit_shifts_ref[mode] == bit, occupation_ref[mode], 0.0)
        weights.append(weight)
    if bits > 1:
        odd = odd_ref[0] == 1
        low, high = weights[-2:]
        weights[-2:] = [jnp.where(odd, low, high), jnp.where(odd, high, low)]
    return weights


def gather_kernel(distances, place_ref, *refs):
    pieces, out_ref, sems = refs[:distances], refs[distances], refs[distances + 1]
    count = pieces[0].shape[0]
    per = out_ref.shape[0] // distances
    copies = []
    for distance, piece in enumerate(pieces):
        rows = pl.ds((place_ref[0] ^ distance) * per, count)
        copies.append(pltpu.make_async_copy(piece, out_ref.at[rows], sems.at[distance]))
        copies[-1].start()
    for copy in copies:
        copy.wait()


def place_first(place, pieces, energies):
    own = pieces[0].shape[1:]
    return pl.pallas_call(
        functools.partial(gather_kernel, len(pieces)),
        out_shape=jax.ShapeDtypeStruct((len(pieces) * energies, *own), jnp.bfloat16),
        in_specs=[SMEM] + [VMEM] * len(pieces),
        out_specs=ANY,
        scratch_shapes=[pltpu.SemaphoreType.DMA((len(pieces),))],
        name="place_first",
    )(place, *in_vmem(pieces))


def last_kernel(
    terms, energies, first, place_ref, odd_ref, bit_shifts_ref, occupation_ref, *refs
):
    arrived, (_, out_ref, result, sems) = refs[:terms], refs[terms:]
    weights = weights_of(terms, odd_ref, bit_shifts_ref, occupation_ref)
    distances, count = result.shape[:2]
    stores = []
    for d in range(distances):
        for e in range(count):
            total = weights[0] * arrived[0][d, e].astype(jnp.float32)
            for weight, term in zip(weights[1:], arrived[1:]):
                total += weight * term[d, e].astype(jnp.float32)
            result[d, e] = total.astype(jnp.bfloat16)
            row = (place_ref[0] ^ d) * energies + first + e
            store = pltpu.make_async_copy(result.at[d, e], out_ref.at[row], sems.at[d, e])
            store.start()
            stores.append(store)
    for store in stores:
        store.wait()


def place_second(scalars, arrived, out, energies, first):
    shape, terms = arrived[0].shape, len(arrived)
    return pl.pallas_call(
        functools.partial(last_kernel, terms, energies, first),
        out_shape=jax.ShapeDtypeStruct(out.shape, out.dtype),
        in_specs=[SMEM] * len(scalars) + [VMEM] * terms + [ANY],
        out_specs=ANY,
        scratch_shapes=[
            pltpu.VMEM(shape, jnp.bfloat16),
            pltpu.SemaphoreType.DMA(shape[:2]),
        ],
        input_output_aliases={len(scalars) + terms: 0},
        name="place_second",
    )(*scalars, *in_vmem(arrived), out)


def stack_kernel(distances, *refs):
    pieces, out_ref, sems = refs[:distances], refs[distances], refs[distances + 1]
    copies = []
    for distance, piece in enumerate(pieces):
        copies.append(pltpu.make_async_copy(piece, out_ref.at[distance], sems.at[distance]))
        copies[-1].start()
    for copy in copies:
        copy.wait()


def stack(pieces):
    return pl.pallas_call(
        functools.partial(stack_kernel, len(pieces)),
        out_shape=jax.ShapeDtypeStruct((len(pieces), *pieces[0].shape), jnp.bfloat16),
        in_specs=[VMEM] * len(pieces),
        out_specs=ANY,
        scratch_shapes=[pltpu.SemaphoreType.DMA((len(pieces),))],
        name="stack",
    )(*in_vmem(pieces))


def term_masks(count):
    bits = count.bit_length() - 1
    masks = [(2**bit, 2**bit) for bit in range(bits)]
    if bits > 1:
        low, high = 2 ** (bits - 2), 2 ** (bits - 1)
        masks[-2:] = [(low, high), (high, low)]
    return masks


def oddness(window, count):
    bits = count.bit_length() - 1
    return (window >> (bits - 1) ^ window >> (bits - 2)) & 1 if bits > 1 else window & 0


def exchange(value, term):
    count = lax.axis_size("win")
    masks = term_masks(count)[term]
    pairs = [(source, source ^ masks[oddness(source, count)]) for source in range(count)]
    return lax.ppermute(value, "win", pairs)


def on_device(retarded, sigma_in, bit_shifts, occupation, neighbors, coupling):
    energies, blocks = retarded.shape[:2]
    atoms = lax.axis_size("atom")
    windows = lax.axis_size("win")
    terms = len(term_masks(windows))
    half = energies // 2
    rest = energies - half
    cut = blocks // 2
    place = lax.axis_index("atom").astype(jnp.int32).reshape(1)
    odd = oddness(lax.axis_index("win"), windows).astype(jnp.int32).reshape(1)
    table = neighbors.T
    begun = lesser_begin(retarded, sigma_in, 0, half, cut)
    arrived_begun = exchange(begun, terms - 2)
    ended, lesser_a = lesser_rest(retarded, sigma_in, begun, 0, half)
    arrived_ended = exchange(ended, terms - 2)
    arrived_a = {}
    for term in reversed(range(terms)):
        if term != terms - 2:
            arrived_a[term] = [exchange(lesser_a, term)]
    arrived_a[terms - 2] = [arrived_begun, arrived_ended]

    coupled_b = lesser_couple(
        place, table, coupling, retarded, sigma_in, half, rest, atoms
    )
    exchanged_b = [coupled_b[0]]
    for distance in range(1, atoms):
        exchanged_b.append(flip(coupled_b[distance], "atom", distance))
    exchanged_b = stack(exchanged_b)
    arrived_b = {}
    for term in range(terms):
        arrived_b[term] = exchange(exchanged_b, term)

    coupled_a = sum_couple(
        (place, odd, bit_shifts, occupation, table),
        coupling,
        [arrived_a[term] for term in range(terms)],
        atoms,
    )
    exchanged_a = [coupled_a[0]]
    for distance in range(1, atoms):
        exchanged_a.append(flip(coupled_a[distance], "atom", distance))
    out = place_first(place, exchanged_a, energies)
    arrived_b = [arrived_b[term] for term in range(terms)]
    scalars = (place, odd, bit_shifts, occupation)
    return place_second(scalars, arrived_b, out, energies, half)


def solution(mesh):
    return jax.shard_map(
        on_device,
        mesh=mesh,
        in_specs=(
            P(("win", "atom"), None, None, None, None),
            P(("win", "atom"), None, None, None, None),
            P(),
            P(),
            P(),
            P(),
        ),
        out_specs=P("win", "atom", None, None, None),
        check_vma=False,
    )
```

```python
import functools
import math

import jax
import jax.numpy as jnp
from jax import lax
from jax.experimental import pallas as pl
from jax.experimental.pallas import tpu as pltpu
from jax.sharding import PartitionSpec as P


SMEM = pl.BlockSpec(memory_space=pltpu.SMEM)
VMEM = pl.BlockSpec(memory_space=pltpu.VMEM)
ANY = pl.BlockSpec(memory_space=pl.ANY)
UNROLL = 8
GROUP = 4
RESIDENT_BYTES = 1600 * 1024


def flip(value, axis, mask):
    pairs = [(source, source ^ mask) for source in range(lax.axis_size(axis))]
    return lax.ppermute(value, axis, pairs)


def contract(left, right, dims):
    return lax.dot_general(
        left, right, (dims, ((), ())), preferred_element_type=jnp.float32
    )


def over_blocks(count, step):
    chunk = math.gcd(count, UNROLL)
    if count == chunk:
        for block in range(count):
            step(block)
        return

    @pl.loop(0, count // chunk)
    def _(outer):
        for inner in range(chunk):
            step(outer * chunk + inner)


def kept(shape):
    if math.prod(shape) * 2 > RESIDENT_BYTES // 2:
        return jax.ShapeDtypeStruct(shape, jnp.bfloat16)
    return pltpu.VMEM(shape, jnp.bfloat16)


def in_vmem(arrays):
    if sum(array.size * array.dtype.itemsize for array in arrays) > RESIDENT_BYTES:
        return arrays
    return [pltpu.with_memory_space_constraint(array, pltpu.VMEM) for array in arrays]


def start_loads(first, count, blocks, retarded_ref, sigma_ref, green, sigma, sems):
    loads = []
    for i, (e, b) in enumerate((e, b) for e in range(count) for b in blocks):
        pair = (
            pltpu.make_async_copy(retarded_ref.at[first + e, b], green.at[i], sems.at[0, i]),
            pltpu.make_async_copy(sigma_ref.at[first + e, b], sigma.at[i], sems.at[1, i]),
        )
        for copy in pair:
            copy.start()
        loads.append(pair)
    return loads


def lesser_items(loads, green, sigma, items):
    for i in items:
        for copy in loads[i]:
            copy.wait()
    for i in items:
        both = lesser_of(green[i, 0], green[i, 1], sigma[i, 0], sigma[i, 1])
        yield i, both.astype(jnp.bfloat16)


def lesser_of(real, imag, sigma_real, sigma_imag):
    left = jnp.concatenate([real, imag], axis=1)
    right = jnp.concatenate(
        [
            jnp.concatenate([sigma_real, sigma_imag], axis=1),
            jnp.concatenate([-sigma_imag, sigma_real], axis=1),
        ],
        axis=0,
    )
    product = contract(left, right, ((1,), (0,))).astype(jnp.bfloat16)
    flipped = jnp.concatenate(
        [
            jnp.concatenate([real, -imag], axis=1),
            jnp.concatenate([imag, real], axis=1),
        ],
        axis=0,
    )
    return contract(product, flipped, ((1,), (1,)))


def bend(coupling_ref, both, bent_ref, block):
    directions, size, _ = coupling_ref.shape
    stacked = coupling_ref[...].reshape(directions * size, size)
    bent = contract(stacked, both, ((1,), (0,))).astype(jnp.bfloat16)
    for direction in range(directions):
        rows = bent[direction * size : (direction + 1) * size]
        bent_ref[block, direction, 0] = rows[:, :size]
        bent_ref[block, direction, 1] = rows[:, size:]


def unbend(place_ref, neighbors_ref, coupling_ref, bent_ref, out_refs, energy):
    directions, size, _ = coupling_ref.shape
    wide = jnp.concatenate([coupling_ref[d] for d in range(directions)], axis=1)
    own = out_refs[0].shape[1]
    for distance, out_ref in enumerate(out_refs):
        for at in range(own):
            block = (place_ref[0] ^ distance) * own + at
            source = [neighbors_ref[d, block] for d in range(directions)]
            left = jnp.concatenate(
                [
                    jnp.concatenate(
                        [bent_ref[source[d], d, part] for d in range(directions)], axis=1
                    )
                    for part in range(2)
                ],
                axis=0,
            )
            total = contract(left, wide, ((1,), (1,))).astype(jnp.bfloat16)
            out_ref[energy, at, 0] = total[:size]
            out_ref[energy, at, 1] = total[size:]


def lesser_kernel(first, cut, retarded_ref, sigma_ref, lesser_ref, green, sigma, sems):
    count, blocks, _, size, _ = lesser_ref.shape
    loads = start_loads(
        first, count, range(cut, cut + blocks), retarded_ref, sigma_ref, green, sigma, sems
    )
    for i, both in lesser_items(loads, green, sigma, range(len(loads))):
        for part in range(2):
            lesser_ref[i // blocks, i % blocks, part] = both[:, part * size : (part + 1) * size]


def lesser_rest_kernel(first, *refs):
    retarded_ref, sigma_ref, begun_ref, rest_ref, whole_ref, green, sigma, sems = refs
    count, blocks, _, size, _ = rest_ref.shape
    cut = begun_ref.shape[1]
    loads = start_loads(
        first, count, range(cut, cut + blocks), retarded_ref, sigma_ref, green, sigma, sems
    )
    whole_ref[:, :cut] = begun_ref[...]
    for i, both in lesser_items(loads, green, sigma, range(len(loads))):
        for part in range(2):
            half = both[:, part * size : (part + 1) * size]
            rest_ref[i // blocks, i % blocks, part] = half
            whole_ref[i // blocks, cut + i % blocks, part] = half


def lesser_scratch(count, blocks, own):
    slots = pltpu.VMEM((count * blocks, *own), jnp.bfloat16)
    return [slots, slots, pltpu.SemaphoreType.DMA((2, count * blocks))]


def lesser_cost(count, blocks, size):
    return pl.CostEstimate(
        flops=count * blocks * 16 * size**3,
        bytes_accessed=count * blocks * 12 * size**2,
        transcendentals=0,
    )


def lesser_begin(retarded, sigma_in, first, count, cut):
    own = retarded.shape[2:]
    return pl.pallas_call(
        functools.partial(lesser_kernel, first, 0),
        out_shape=kept((count, cut, *own)),
        in_specs=[ANY, ANY],
        out_specs=VMEM,
        scratch_shapes=lesser_scratch(count, cut, own),
        cost_estimate=lesser_cost(count, cut, own[-1]),
        name="lesser_begin",
    )(retarded, sigma_in)


def lesser_rest(retarded, sigma_in, begun, first, count):
    blocks, *own = retarded.shape[1:]
    rest = blocks - begun.shape[1]
    return pl.pallas_call(
        functools.partial(lesser_rest_kernel, first),
        out_shape=[kept((count, rest, *own)), kept((count, blocks, *own))],
        in_specs=[ANY, ANY, VMEM],
        out_specs=[VMEM, VMEM],
        scratch_shapes=lesser_scratch(count, rest, own),
        cost_estimate=lesser_cost(count, rest, own[-1]),
        name="lesser_rest",
    )(retarded, sigma_in, *in_vmem([begun]))


def lesser_couple_kernel(first, place_ref, neighbors_ref, coupling_ref, *refs):
    retarded_ref, sigma_ref, *out_refs, bent_ref, made, green, sigma, sems = refs
    blocks = retarded_ref.shape[1]
    count = out_refs[0].shape[0]
    loads = start_loads(
        first, count, range(blocks), retarded_ref, sigma_ref, green, sigma, sems
    )
    for start in range(0, len(loads), GROUP):
        group = range(start, min(start + GROUP, len(loads)))
        for i, both in lesser_items(loads, green, sigma, group):
            made[i % GROUP] = both
        for i in group:
            bend(coupling_ref, made[i % GROUP], bent_ref, i % blocks)
            if i % blocks == blocks - 1:
                unbend(place_ref, neighbors_ref, coupling_ref, bent_ref, out_refs, i // blocks)


def lesser_couple(place, neighbors, coupling, retarded, sigma_in, first, count, atoms):
    blocks, *own = retarded.shape[1:]
    directions, size, _ = coupling.shape
    return pl.pallas_call(
        functools.partial(lesser_couple_kernel, first),
        out_shape=[kept((count, blocks // atoms, *own))] * atoms,
        in_specs=[SMEM, SMEM, VMEM, ANY, ANY],
        out_specs=[VMEM] * atoms,
        scratch_shapes=[
            pltpu.VMEM((blocks, directions, *own), jnp.bfloat16),
            pltpu.VMEM((GROUP, size, own[0] * size), jnp.bfloat16),
        ]
        + lesser_scratch(count, blocks, own),
        cost_estimate=pl.CostEstimate(
            flops=count * blocks * (16 + directions * 8) * size**3,
            bytes_accessed=count * blocks * 12 * size**2,
            transcendentals=0,
        ),
        name="lesser_couple",
    )(place, neighbors, coupling, retarded, sigma_in)


def sum_couple_kernel(
    widths, place_ref, odd_ref, bit_shifts_ref, occupation_ref, neighbors_ref, coupling_ref, *refs
):
    taken = sum(widths)
    arrived, weights_ref, out_refs = list(refs[:taken]), refs[taken], refs[taken + 1 : -1]
    bent_ref = refs[-1]
    terms = [[arrived.pop(0) for _ in range(width)] for width in widths]
    weights = weights_of(len(terms), odd_ref, bit_shifts_ref, occupation_ref)
    for at, weight in enumerate(weights):
        weights_ref[at] = jnp.full(weights_ref.shape[1:], weight, jnp.float32)
    span = bent_ref.shape[0] // max(widths)
    for piece in range(max(widths)):

        def one(at, piece=piece):
            parts = []
            for part in range(2):
                total = None
                for weight, term in zip(weights, terms):
                    block = at if len(term) > 1 else piece * span + at
                    value = term[piece % len(term)][0, block, part].astype(jnp.float32)
                    total = weight * value if total is None else total + weight * value
                parts.append(total.astype(jnp.bfloat16))
            bend(coupling_ref, jnp.concatenate(parts, axis=1), bent_ref, piece * span + at)

        over_blocks(span, one)
    unbend(place_ref, neighbors_ref, coupling_ref, bent_ref, out_refs, 0)


def sum_couple(scalars, coupling, terms, atoms):
    count, blocks, *own = terms[0][0].shape
    directions = coupling.shape[0]
    arrays = [array for term in terms for array in term]
    return pl.pallas_call(
        functools.partial(sum_couple_kernel, [len(term) for term in terms]),
        out_shape=[pltpu.VMEM((len(terms), 8, own[-1]), jnp.float32)]
        + [jax.ShapeDtypeStruct((count, blocks // atoms, *own), jnp.bfloat16)] * atoms,
        grid=(count,),
        in_specs=[SMEM] * len(scalars)
        + [VMEM]
        + [pl.BlockSpec((1, *array.shape[1:]), lambda e: (e, 0, 0, 0, 0)) for array in arrays],
        out_specs=[VMEM]
        + [
            pl.BlockSpec((1, blocks // atoms, *own), lambda e: (e, 0, 0, 0, 0))
            for _ in range(atoms)
        ],
        scratch_shapes=[pltpu.VMEM((blocks, directions, *own), jnp.bfloat16)],
        cost_estimate=pl.CostEstimate(
            flops=count * blocks * directions * 8 * own[-1] ** 3,
            bytes_accessed=count * blocks * 12 * own[-1] ** 2,
            transcendentals=0,
        ),
        name="sum_couple",
    )(*scalars, coupling, *arrays)


def weights_of(bits, odd_ref, bit_shifts_ref, occupation_ref):
    weights = []
    for bit in range(bits):
        weight = jnp.float32(0)
        for mode in range(bit_shifts_ref.shape[0]):
            weight += jnp.where(bit_shifts_ref[mode] == bit, occupation_ref[mode], 0.0)
        weights.append(weight)
    if bits > 1:
        odd = odd_ref[0] == 1
        low, high = weights[-2:]
        weights[-2:] = [jnp.where(odd, low, high), jnp.where(odd, high, low)]
    return weights


def gather_kernel(distances, place_ref, *refs):
    pieces, out_ref, sems = refs[:distances], refs[distances], refs[distances + 1]
    count = pieces[0].shape[0]
    per = out_ref.shape[0] // distances
    copies = []
    for distance, piece in enumerate(pieces):
        rows = pl.ds((place_ref[0] ^ distance) * per, count)
        copies.append(pltpu.make_async_copy(piece, out_ref.at[rows], sems.at[distance]))
        copies[-1].start()
    for copy in copies:
        copy.wait()


def place_first(place, pieces, energies):
    own = pieces[0].shape[1:]
    return pl.pallas_call(
        functools.partial(gather_kernel, len(pieces)),
        out_shape=jax.ShapeDtypeStruct((len(pieces) * energies, *own), jnp.bfloat16),
        in_specs=[SMEM] + [VMEM] * len(pieces),
        out_specs=ANY,
        scratch_shapes=[pltpu.SemaphoreType.DMA((len(pieces),))],
        name="place_first",
    )(place, *in_vmem(pieces))


def last_kernel(terms, energies, first, weights_ref, *refs):
    arrived, (_, out_ref, result, sems) = refs[:terms], refs[terms:]
    weights = [weights_ref[at, :1] for at in range(terms)]
    place = lax.axis_index("atom")
    distances, count = result.shape[:2]
    stores = []
    for d in range(distances):
        for e in range(count):
            total = weights[0] * arrived[0][d, e].astype(jnp.float32)
            for weight, term in zip(weights[1:], arrived[1:]):
                total += weight * term[d, e].astype(jnp.float32)
            result[d, e] = total.astype(jnp.bfloat16)
            row = (place ^ d) * energies + first + e
            store = pltpu.make_async_copy(result.at[d, e], out_ref.at[row], sems.at[d, e])
            store.start()
            stores.append(store)
    for store in stores:
        store.wait()


def place_second(weights, arrived, out, energies, first):
    shape, terms = arrived[0].shape, len(arrived)
    return pl.pallas_call(
        functools.partial(last_kernel, terms, energies, first),
        out_shape=jax.ShapeDtypeStruct(out.shape, out.dtype),
        in_specs=[VMEM] * (terms + 1) + [ANY],
        out_specs=ANY,
        scratch_shapes=[
            pltpu.VMEM(shape, jnp.bfloat16),
            pltpu.SemaphoreType.DMA(shape[:2]),
        ],
        input_output_aliases={terms + 1: 0},
        name="place_second",
    )(*in_vmem([weights]), *in_vmem(arrived), out)


def stack_kernel(distances, *refs):
    pieces, out_ref, sems = refs[:distances], refs[distances], refs[distances + 1]
    copies = []
    for distance, piece in enumerate(pieces):
        copies.append(pltpu.make_async_copy(piece, out_ref.at[distance], sems.at[distance]))
        copies[-1].start()
    for copy in copies:
        copy.wait()


def stack(pieces):
    return pl.pallas_call(
        functools.partial(stack_kernel, len(pieces)),
        out_shape=jax.ShapeDtypeStruct((len(pieces), *pieces[0].shape), jnp.bfloat16),
        in_specs=[VMEM] * len(pieces),
        out_specs=ANY,
        scratch_shapes=[pltpu.SemaphoreType.DMA((len(pieces),))],
        name="stack",
    )(*in_vmem(pieces))


def term_masks(count):
    bits = count.bit_length() - 1
    masks = [(2**bit, 2**bit) for bit in range(bits)]
    if bits > 1:
        low, high = 2 ** (bits - 2), 2 ** (bits - 1)
        masks[-2:] = [(low, high), (high, low)]
    return masks


def oddness(window, count):
    bits = count.bit_length() - 1
    return (window >> (bits - 1) ^ window >> (bits - 2)) & 1 if bits > 1 else window & 0


def exchange(value, term):
    count = lax.axis_size("win")
    masks = term_masks(count)[term]
    pairs = [(source, source ^ masks[oddness(source, count)]) for source in range(count)]
    return lax.ppermute(value, "win", pairs)


def on_device(retarded, sigma_in, bit_shifts, occupation, neighbors, coupling):
    energies, blocks = retarded.shape[:2]
    atoms = lax.axis_size("atom")
    windows = lax.axis_size("win")
    terms = len(term_masks(windows))
    half = energies // 2
    rest = energies - half
    cut = blocks // 2
    place = lax.axis_index("atom").astype(jnp.int32).reshape(1)
    odd = oddness(lax.axis_index("win"), windows).astype(jnp.int32).reshape(1)
    table = neighbors.T
    begun = lesser_begin(retarded, sigma_in, 0, half, cut)
    arrived_begun = exchange(begun, terms - 2)
    ended, lesser_a = lesser_rest(retarded, sigma_in, begun, 0, half)
    arrived_ended = exchange(ended, terms - 2)
    arrived_a = {}
    for term in reversed(range(terms)):
        if term != terms - 2:
            arrived_a[term] = [exchange(lesser_a, term)]
    arrived_a[terms - 2] = [arrived_begun, arrived_ended]

    coupled_b = lesser_couple(
        place, table, coupling, retarded, sigma_in, half, rest, atoms
    )
    exchanged_b = [coupled_b[0]]
    for distance in range(1, atoms):
        exchanged_b.append(flip(coupled_b[distance], "atom", distance))
    exchanged_b = stack(exchanged_b)
    arrived_b = {}
    for term in range(terms):
        arrived_b[term] = exchange(exchanged_b, term)

    weights, *coupled_a = sum_couple(
        (place, odd, bit_shifts, occupation, table),
        coupling,
        [arrived_a[term] for term in range(terms)],
        atoms,
    )
    exchanged_a = [coupled_a[0]]
    for distance in range(1, atoms):
        exchanged_a.append(flip(coupled_a[distance], "atom", distance))
    out = place_first(place, exchanged_a, energies)
    arrived_b = [arrived_b[term] for term in range(terms)]
    return place_second(weights, arrived_b, out, energies, half)


def solution(mesh):
    return jax.shard_map(
        on_device,
        mesh=mesh,
        in_specs=(
            P(("win", "atom"), None, None, None, None),
            P(("win", "atom"), None, None, None, None),
            P(),
            P(),
            P(),
            P(),
        ),
        out_specs=P("win", "atom", None, None, None),
        check_vma=False,
    )
```

```python
import functools
import math

import jax
import jax.numpy as jnp
from jax import lax
from jax.experimental import pallas as pl
from jax.experimental.pallas import tpu as pltpu
from jax.sharding import PartitionSpec as P


SMEM = pl.BlockSpec(memory_space=pltpu.SMEM)
VMEM = pl.BlockSpec(memory_space=pltpu.VMEM)
ANY = pl.BlockSpec(memory_space=pl.ANY)
HBM = pl.BlockSpec(memory_space=pltpu.HBM)
UNROLL = 8
GROUP = 4
RESIDENT_BYTES = 1600 * 1024
PARAMS = pltpu.CompilerParams(vmem_limit_bytes=40 * 2**20)


def flip(value, axis, mask):
    pairs = [(source, source ^ mask) for source in range(lax.axis_size(axis))]
    return lax.ppermute(value, axis, pairs)


def contract(left, right, dims):
    return lax.dot_general(
        left, right, (dims, ((), ())), preferred_element_type=jnp.float32
    )


def over_blocks(count, step):
    chunk = count if count <= UNROLL else math.gcd(count, UNROLL)
    if count == chunk:
        for block in range(count):
            step(block)
        return

    @pl.loop(0, count // chunk)
    def _(outer):
        for inner in range(chunk):
            step(outer * chunk + inner)


def kept(shape):
    if math.prod(shape) * 2 > RESIDENT_BYTES // 2:
        return jax.ShapeDtypeStruct(shape, jnp.bfloat16)
    return pltpu.VMEM(shape, jnp.bfloat16)


def in_vmem(arrays):
    if sum(array.size * array.dtype.itemsize for array in arrays) > RESIDENT_BYTES:
        return arrays
    return [pltpu.with_memory_space_constraint(array, pltpu.VMEM) for array in arrays]


def start_loads(first, count, blocks, retarded_ref, sigma_ref, green, sigma, sems):
    loads = []
    for i, (e, b) in enumerate((e, b) for e in range(count) for b in blocks):
        pair = (
            pltpu.make_async_copy(retarded_ref.at[first + e, b], green.at[i], sems.at[0, i]),
            pltpu.make_async_copy(sigma_ref.at[first + e, b], sigma.at[i], sems.at[1, i]),
        )
        for copy in pair:
            copy.start()
        loads.append(pair)
    return loads


def lesser_items(loads, green, sigma, items):
    for i in items:
        for copy in loads[i]:
            copy.wait()
    products = [product_of(green[i], sigma[i]) for i in items]
    for i, product in zip(items, products):
        yield i, lesser_of(product, green[i]).astype(jnp.bfloat16)


def product_of(green, sigma):
    right = jnp.concatenate(
        [
            jnp.concatenate([sigma[0], sigma[1]], axis=1),
            jnp.concatenate([-sigma[1], sigma[0]], axis=1),
        ],
        axis=0,
    )
    left = jnp.concatenate([green[0], green[1]], axis=1)
    return contract(left, right, ((1,), (0,))).astype(jnp.bfloat16)


def lesser_of(product, green):
    flipped = jnp.concatenate(
        [
            jnp.concatenate([green[0], -green[1]], axis=1),
            jnp.concatenate([green[1], green[0]], axis=1),
        ],
        axis=0,
    )
    return contract(product, flipped, ((1,), (1,)))


def bend(coupling_ref, both, bent_ref, block):
    directions, size, _ = coupling_ref.shape
    stacked = coupling_ref[...].reshape(directions * size, size)
    bent = contract(stacked, both, ((1,), (0,))).astype(jnp.bfloat16)
    for direction in range(directions):
        rows = bent[direction * size : (direction + 1) * size]
        bent_ref[block, direction, 0] = rows[:, :size]
        bent_ref[block, direction, 1] = rows[:, size:]


def unbend(place_ref, neighbors_ref, coupling_ref, bent_ref, out_refs, energy):
    directions, size, _ = coupling_ref.shape
    wide = jnp.concatenate([coupling_ref[d] for d in range(directions)], axis=1)
    own = out_refs[0].shape[1]
    for distance, out_ref in enumerate(out_refs):
        for at in range(own):
            block = (place_ref[0] ^ distance) * own + at
            source = [neighbors_ref[d, block] for d in range(directions)]
            left = jnp.concatenate(
                [
                    jnp.concatenate(
                        [bent_ref[source[d], d, part] for d in range(directions)], axis=1
                    )
                    for part in range(2)
                ],
                axis=0,
            )
            total = contract(left, wide, ((1,), (1,))).astype(jnp.bfloat16)
            out_ref[energy, at, 0] = total[:size]
            out_ref[energy, at, 1] = total[size:]


def lesser_kernel(first, cut, retarded_ref, sigma_ref, lesser_ref, green, sigma, sems):
    count, blocks, _, size, _ = lesser_ref.shape
    loads = start_loads(
        first, count, range(cut, cut + blocks), retarded_ref, sigma_ref, green, sigma, sems
    )
    for i, both in lesser_items(loads, green, sigma, range(len(loads))):
        for part in range(2):
            lesser_ref[i // blocks, i % blocks, part] = both[:, part * size : (part + 1) * size]


def lesser_rest_kernel(first, *refs):
    retarded_ref, sigma_ref, begun_ref, rest_ref, whole_ref, green, sigma, sems = refs
    count, blocks, _, size, _ = rest_ref.shape
    cut = begun_ref.shape[1]
    loads = start_loads(
        first, count, range(cut, cut + blocks), retarded_ref, sigma_ref, green, sigma, sems
    )
    whole_ref[:, :cut] = begun_ref[...]
    for i, both in lesser_items(loads, green, sigma, range(len(loads))):
        for part in range(2):
            half = both[:, part * size : (part + 1) * size]
            rest_ref[i // blocks, i % blocks, part] = half
            whole_ref[i // blocks, cut + i % blocks, part] = half


def lesser_scratch(count, blocks, own):
    slots = pltpu.VMEM((count * blocks, *own), jnp.bfloat16)
    return [slots, slots, pltpu.SemaphoreType.DMA((2, count * blocks))]


def lesser_cost(count, blocks, size):
    return pl.CostEstimate(
        flops=count * blocks * 16 * size**3,
        bytes_accessed=count * blocks * 12 * size**2,
        transcendentals=0,
    )


def lesser_begin(retarded, sigma_in, first, count, cut):
    own = retarded.shape[2:]
    return pl.pallas_call(
        functools.partial(lesser_kernel, first, 0),
        out_shape=kept((count, cut, *own)),
        in_specs=[HBM, HBM],
        out_specs=VMEM,
        scratch_shapes=lesser_scratch(count, cut, own),
        cost_estimate=lesser_cost(count, cut, own[-1]),
        compiler_params=PARAMS,
        name="lesser_begin",
    )(retarded, sigma_in)


def lesser_rest(retarded, sigma_in, begun, first, count):
    blocks, *own = retarded.shape[1:]
    rest = blocks - begun.shape[1]
    return pl.pallas_call(
        functools.partial(lesser_rest_kernel, first),
        out_shape=[kept((count, rest, *own)), kept((count, blocks, *own))],
        in_specs=[HBM, HBM, VMEM],
        out_specs=[VMEM, VMEM],
        scratch_shapes=lesser_scratch(count, rest, own),
        cost_estimate=lesser_cost(count, rest, own[-1]),
        compiler_params=PARAMS,
        name="lesser_rest",
    )(retarded, sigma_in, *in_vmem([begun]))


def lesser_couple_kernel(first, place_ref, neighbors_ref, coupling_ref, *refs):
    retarded_ref, sigma_ref, *out_refs, bent_ref, made, green, sigma, sems = refs
    blocks = retarded_ref.shape[1]
    count = out_refs[0].shape[0]
    loads = start_loads(
        first, count, range(blocks), retarded_ref, sigma_ref, green, sigma, sems
    )
    for start in range(0, len(loads), GROUP):
        group = range(start, min(start + GROUP, len(loads)))
        for i, both in lesser_items(loads, green, sigma, group):
            made[i % GROUP] = both
        for i in group:
            bend(coupling_ref, made[i % GROUP], bent_ref, i % blocks)
            if i % blocks == blocks - 1:
                unbend(place_ref, neighbors_ref, coupling_ref, bent_ref, out_refs, i // blocks)


def lesser_couple(place, neighbors, coupling, retarded, sigma_in, first, count, atoms):
    blocks, *own = retarded.shape[1:]
    directions, size, _ = coupling.shape
    return pl.pallas_call(
        functools.partial(lesser_couple_kernel, first),
        out_shape=[kept((count, blocks // atoms, *own))] * atoms,
        in_specs=[SMEM, SMEM, VMEM, HBM, HBM],
        out_specs=[VMEM] * atoms,
        scratch_shapes=[
            pltpu.VMEM((blocks, directions, *own), jnp.bfloat16),
            pltpu.VMEM((GROUP, size, own[0] * size), jnp.bfloat16),
        ]
        + lesser_scratch(count, blocks, own),
        cost_estimate=pl.CostEstimate(
            flops=count * blocks * (16 + directions * 8) * size**3,
            bytes_accessed=count * blocks * 12 * size**2,
            transcendentals=0,
        ),
        compiler_params=PARAMS,
        name="lesser_couple",
    )(place, neighbors, coupling, retarded, sigma_in)


def sum_couple_kernel(
    widths, place_ref, odd_ref, bit_shifts_ref, occupation_ref, neighbors_ref, coupling_ref, *refs
):
    taken = sum(widths)
    arrived, weights_ref, out_refs = list(refs[:taken]), refs[taken], refs[taken + 1 : -1]
    bent_ref = refs[-1]
    terms = [[arrived.pop(0) for _ in range(width)] for width in widths]
    weights = weights_of(len(terms), odd_ref, bit_shifts_ref, occupation_ref)
    for at, weight in enumerate(weights):
        weights_ref[at] = jnp.full(weights_ref.shape[1:], weight, jnp.float32)
    cuts = [piece.shape[1] for piece in max(terms, key=len)]
    for piece, span in enumerate(cuts):
        before = sum(cuts[:piece])

        def one(at, piece=piece, before=before):
            parts = []
            for part in range(2):
                total = None
                for weight, term in zip(weights, terms):
                    block = at if len(term) > 1 else before + at
                    value = term[piece % len(term)][0, block, part].astype(jnp.float32)
                    total = weight * value if total is None else total + weight * value
                parts.append(total.astype(jnp.bfloat16))
            bend(coupling_ref, jnp.concatenate(parts, axis=1), bent_ref, before + at)

        over_blocks(span, one)
    unbend(place_ref, neighbors_ref, coupling_ref, bent_ref, out_refs, 0)


def sum_couple(scalars, coupling, terms, atoms):
    count, blocks, *own = min(terms, key=len)[0].shape
    directions = coupling.shape[0]
    arrays = [array for term in terms for array in term]
    return pl.pallas_call(
        functools.partial(sum_couple_kernel, [len(term) for term in terms]),
        out_shape=[pltpu.VMEM((len(terms), 8, own[-1]), jnp.float32)]
        + [jax.ShapeDtypeStruct((count, blocks // atoms, *own), jnp.bfloat16)] * atoms,
        grid=(count,),
        in_specs=[SMEM] * len(scalars)
        + [VMEM]
        + [pl.BlockSpec((1, *array.shape[1:]), lambda e: (e, 0, 0, 0, 0)) for array in arrays],
        out_specs=[VMEM]
        + [
            pl.BlockSpec((1, blocks // atoms, *own), lambda e: (e, 0, 0, 0, 0))
            for _ in range(atoms)
        ],
        scratch_shapes=[pltpu.VMEM((blocks, directions, *own), jnp.bfloat16)],
        cost_estimate=pl.CostEstimate(
            flops=count * blocks * directions * 8 * own[-1] ** 3,
            bytes_accessed=count * blocks * 12 * own[-1] ** 2,
            transcendentals=0,
        ),
        compiler_params=PARAMS,
        name="sum_couple",
    )(*scalars, coupling, *arrays)


def weights_of(bits, odd_ref, bit_shifts_ref, occupation_ref):
    weights = []
    for bit in range(bits):
        weight = jnp.float32(0)
        for mode in range(bit_shifts_ref.shape[0]):
            weight += jnp.where(bit_shifts_ref[mode] == bit, occupation_ref[mode], 0.0)
        weights.append(weight)
    if bits > 1:
        odd = odd_ref[0] == 1
        low, high = weights[-2:]
        weights[-2:] = [jnp.where(odd, low, high), jnp.where(odd, high, low)]
    return weights


def gather_kernel(distances, place_ref, *refs):
    pieces, out_ref, sems = refs[:distances], refs[distances], refs[distances + 1]
    count = pieces[0].shape[0]
    per = out_ref.shape[0] // distances
    copies = []
    for distance, piece in enumerate(pieces):
        rows = pl.ds((place_ref[0] ^ distance) * per, count)
        copies.append(pltpu.make_async_copy(piece, out_ref.at[rows], sems.at[distance]))
        copies[-1].start()
    for copy in copies:
        copy.wait()


def place_first(place, pieces, energies):
    own = pieces[0].shape[1:]
    return pl.pallas_call(
        functools.partial(gather_kernel, len(pieces)),
        out_shape=jax.ShapeDtypeStruct((len(pieces) * energies, *own), jnp.bfloat16),
        in_specs=[SMEM] + [VMEM] * len(pieces),
        out_specs=ANY,
        scratch_shapes=[pltpu.SemaphoreType.DMA((len(pieces),))],
        compiler_params=PARAMS,
        name="place_first",
    )(place, *in_vmem(pieces))


def last_kernel(terms, energies, first, weights_ref, *refs):
    arrived, (_, out_ref, result, sems) = refs[:terms], refs[terms:]
    weights = [weights_ref[at, :1] for at in range(terms)]
    place = lax.axis_index("atom")
    distances, count = result.shape[:2]
    stores = []
    for d in range(distances):
        for e in range(count):
            total = weights[0] * arrived[0][d, e].astype(jnp.float32)
            for weight, term in zip(weights[1:], arrived[1:]):
                total += weight * term[d, e].astype(jnp.float32)
            result[d, e] = total.astype(jnp.bfloat16)
            row = (place ^ d) * energies + first + e
            store = pltpu.make_async_copy(result.at[d, e], out_ref.at[row], sems.at[d, e])
            store.start()
            stores.append(store)
    for store in stores:
        store.wait()


def place_second(weights, arrived, out, energies, first):
    shape, terms = arrived[0].shape, len(arrived)
    return pl.pallas_call(
        functools.partial(last_kernel, terms, energies, first),
        out_shape=jax.ShapeDtypeStruct(out.shape, out.dtype),
        in_specs=[VMEM] * (terms + 1) + [ANY],
        out_specs=ANY,
        scratch_shapes=[
            pltpu.VMEM(shape, jnp.bfloat16),
            pltpu.SemaphoreType.DMA(shape[:2]),
        ],
        input_output_aliases={terms + 1: 0},
        compiler_params=PARAMS,
        name="place_second",
    )(*in_vmem([weights]), *in_vmem(arrived), out)


def stack_kernel(distances, *refs):
    pieces, out_ref, sems = refs[:distances], refs[distances], refs[distances + 1]
    copies = []
    for distance, piece in enumerate(pieces):
        copies.append(pltpu.make_async_copy(piece, out_ref.at[distance], sems.at[distance]))
        copies[-1].start()
    for copy in copies:
        copy.wait()


def stack(pieces):
    return pl.pallas_call(
        functools.partial(stack_kernel, len(pieces)),
        out_shape=jax.ShapeDtypeStruct((len(pieces), *pieces[0].shape), jnp.bfloat16),
        in_specs=[VMEM] * len(pieces),
        out_specs=ANY,
        scratch_shapes=[pltpu.SemaphoreType.DMA((len(pieces),))],
        compiler_params=PARAMS,
        name="stack",
    )(*in_vmem(pieces))


def term_masks(count):
    bits = count.bit_length() - 1
    masks = [(2**bit, 2**bit) for bit in range(bits)]
    if bits > 1:
        low, high = 2 ** (bits - 2), 2 ** (bits - 1)
        masks[-2:] = [(low, high), (high, low)]
    return masks


def oddness(window, count):
    bits = count.bit_length() - 1
    return (window >> (bits - 1) ^ window >> (bits - 2)) & 1 if bits > 1 else window & 0


def exchange(value, term):
    count = lax.axis_size("win")
    masks = term_masks(count)[term]
    pairs = [(source, source ^ masks[oddness(source, count)]) for source in range(count)]
    return lax.ppermute(value, "win", pairs)


def on_device(retarded, sigma_in, bit_shifts, occupation, neighbors, coupling):
    energies, blocks = retarded.shape[:2]
    atoms = lax.axis_size("atom")
    windows = lax.axis_size("win")
    terms = len(term_masks(windows))
    half = energies // 2
    rest = energies - half
    cut = blocks * 3 // 8
    place = lax.axis_index("atom").astype(jnp.int32).reshape(1)
    odd = oddness(lax.axis_index("win"), windows).astype(jnp.int32).reshape(1)
    retarded, sigma_in = [
        pltpu.with_memory_space_constraint(array, pltpu.HBM) for array in (retarded, sigma_in)
    ]
    table = neighbors.T
    begun = lesser_begin(retarded, sigma_in, 0, half, cut)
    arrived_begun = exchange(begun, terms - 2)
    ended, lesser_a = lesser_rest(retarded, sigma_in, begun, 0, half)
    arrived_ended = exchange(ended, terms - 2)
    arrived_a = {}
    for term in reversed(range(terms)):
        if term != terms - 2:
            arrived_a[term] = [exchange(lesser_a, term)]
    arrived_a[terms - 2] = [arrived_begun, arrived_ended]

    coupled_b = lesser_couple(
        place, table, coupling, retarded, sigma_in, half, rest, atoms
    )
    exchanged_b = [coupled_b[0]]
    for distance in range(1, atoms):
        exchanged_b.append(flip(coupled_b[distance], "atom", distance))
    exchanged_b = stack(exchanged_b)
    arrived_b = {}
    for term in range(terms):
        arrived_b[term] = exchange(exchanged_b, term)

    weights, *coupled_a = sum_couple(
        (place, odd, bit_shifts, occupation, table),
        coupling,
        [arrived_a[term] for term in range(terms)],
        atoms,
    )
    exchanged_a = [coupled_a[0]]
    for distance in range(1, atoms):
        exchanged_a.append(flip(coupled_a[distance], "atom", distance))
    out = place_first(place, exchanged_a, energies)
    arrived_b = [arrived_b[term] for term in range(terms)]
    return place_second(weights, arrived_b, out, energies, half)


def solution(mesh):
    return jax.shard_map(
        on_device,
        mesh=mesh,
        in_specs=(
            P(("win", "atom"), None, None, None, None),
            P(("win", "atom"), None, None, None, None),
            P(),
            P(),
            P(),
            P(),
        ),
        out_specs=P("win", "atom", None, None, None),
        check_vma=False,
    )
```

```python
import functools
import math

import jax
import jax.numpy as jnp
from jax import lax
from jax.experimental import pallas as pl
from jax.experimental.pallas import tpu as pltpu
from jax.sharding import PartitionSpec as P


SMEM = pl.BlockSpec(memory_space=pltpu.SMEM)
VMEM = pl.BlockSpec(memory_space=pltpu.VMEM)
ANY = pl.BlockSpec(memory_space=pl.ANY)
HBM = pl.BlockSpec(memory_space=pltpu.HBM)
UNROLL = 8
GROUP = 4
NEARS = 4
RESIDENT_BYTES = 1600 * 1024
PARAMS = pltpu.CompilerParams(vmem_limit_bytes=24 * 2**20)


def flip(value, axis, mask):
    pairs = [(source, source ^ mask) for source in range(lax.axis_size(axis))]
    return lax.ppermute(value, axis, pairs)


def contract(left, right, dims):
    return lax.dot_general(
        left, right, (dims, ((), ())), preferred_element_type=jnp.float32
    )


def over_blocks(count, step):
    chunk = count if count <= UNROLL else math.gcd(count, UNROLL)
    if count == chunk:
        for block in range(count):
            step(block)
        return

    @pl.loop(0, count // chunk)
    def _(outer):
        for inner in range(chunk):
            step(outer * chunk + inner)


def kept(shape):
    if math.prod(shape) * 2 > RESIDENT_BYTES // 2:
        return jax.ShapeDtypeStruct(shape, jnp.bfloat16)
    return pltpu.VMEM(shape, jnp.bfloat16)


def in_vmem(arrays):
    if sum(array.size * array.dtype.itemsize for array in arrays) > RESIDENT_BYTES:
        return arrays
    return [pltpu.with_memory_space_constraint(array, pltpu.VMEM) for array in arrays]


def start_loads(first, count, blocks, retarded_ref, sigma_ref, green, sigma, sems):
    loads = []
    for i, (e, b) in enumerate((e, b) for e in range(count) for b in blocks):
        pair = (
            pltpu.make_async_copy(retarded_ref.at[first + e, b], green.at[i], sems.at[0, i]),
            pltpu.make_async_copy(sigma_ref.at[first + e, b], sigma.at[i], sems.at[1, i]),
        )
        for copy in pair:
            copy.start()
        loads.append(pair)
    return loads


def lesser_items(loads, green, sigma, items):
    for i in items:
        for copy in loads[i]:
            copy.wait()
    products = [product_of(green[i], sigma[i]) for i in items]
    for i, product in zip(items, products):
        yield i, lesser_of(product, green[i]).astype(jnp.bfloat16)


def product_of(green, sigma):
    right = jnp.concatenate(
        [
            jnp.concatenate([sigma[0], sigma[1]], axis=1),
            jnp.concatenate([-sigma[1], sigma[0]], axis=1),
        ],
        axis=0,
    )
    left = jnp.concatenate([green[0], green[1]], axis=1)
    return contract(left, right, ((1,), (0,))).astype(jnp.bfloat16)


def lesser_of(product, green):
    flipped = jnp.concatenate(
        [
            jnp.concatenate([green[0], -green[1]], axis=1),
            jnp.concatenate([green[1], green[0]], axis=1),
        ],
        axis=0,
    )
    return contract(product, flipped, ((1,), (1,)))


def bend(coupling_ref, both, bent_ref, block):
    directions, size, _ = coupling_ref.shape
    stacked = coupling_ref[...].reshape(directions * size, size)
    bent = contract(stacked, both, ((1,), (0,))).astype(jnp.bfloat16)
    for direction in range(directions):
        rows = bent[direction * size : (direction + 1) * size]
        bent_ref[block, direction, 0] = rows[:, :size]
        bent_ref[block, direction, 1] = rows[:, size:]


def unbend(place_ref, neighbors_ref, coupling_ref, bent_ref, out_refs, energy):
    directions, size, _ = coupling_ref.shape
    wide = jnp.concatenate([coupling_ref[d] for d in range(directions)], axis=1)
    own = out_refs[0].shape[1]
    for distance, out_ref in enumerate(out_refs):
        for at in range(own):
            block = (place_ref[0] ^ distance) * own + at
            source = [neighbors_ref[d, block] for d in range(directions)]
            left = jnp.concatenate(
                [
                    jnp.concatenate(
                        [bent_ref[source[d], d, part] for d in range(directions)], axis=1
                    )
                    for part in range(2)
                ],
                axis=0,
            )
            total = contract(left, wide, ((1,), (1,))).astype(jnp.bfloat16)
            out_ref[energy, at, 0] = total[:size]
            out_ref[energy, at, 1] = total[size:]


def lesser_kernel(first, cut, retarded_ref, sigma_ref, lesser_ref, green, sigma, sems):
    count, blocks, _, size, _ = lesser_ref.shape
    loads = start_loads(
        first, count, range(cut, cut + blocks), retarded_ref, sigma_ref, green, sigma, sems
    )
    for i, both in lesser_items(loads, green, sigma, range(len(loads))):
        for part in range(2):
            lesser_ref[i // blocks, i % blocks, part] = both[:, part * size : (part + 1) * size]


def lesser_rest_kernel(first, *refs):
    retarded_ref, sigma_ref, begun_ref, rest_ref, whole_ref, green, sigma, sems = refs
    count, blocks, _, size, _ = rest_ref.shape
    cut = begun_ref.shape[1]
    loads = start_loads(
        first, count, range(cut, cut + blocks), retarded_ref, sigma_ref, green, sigma, sems
    )
    whole_ref[:, :cut] = begun_ref[...]
    for i, both in lesser_items(loads, green, sigma, range(len(loads))):
        for part in range(2):
            half = both[:, part * size : (part + 1) * size]
            rest_ref[i // blocks, i % blocks, part] = half
            whole_ref[i // blocks, cut + i % blocks, part] = half


def lesser_scratch(count, blocks, own):
    slots = pltpu.VMEM((count * blocks, *own), jnp.bfloat16)
    return [slots, slots, pltpu.SemaphoreType.DMA((2, count * blocks))]


def lesser_cost(count, blocks, size):
    return pl.CostEstimate(
        flops=count * blocks * 16 * size**3,
        bytes_accessed=count * blocks * 12 * size**2,
        transcendentals=0,
    )


def lesser_begin(retarded, sigma_in, first, count, cut):
    own = retarded.shape[2:]
    return pl.pallas_call(
        functools.partial(lesser_kernel, first, 0),
        out_shape=kept((count, cut, *own)),
        in_specs=[HBM, HBM],
        out_specs=VMEM,
        scratch_shapes=lesser_scratch(count, cut, own),
        cost_estimate=lesser_cost(count, cut, own[-1]),
        compiler_params=PARAMS,
        name="lesser_begin",
    )(retarded, sigma_in)


def lesser_rest(retarded, sigma_in, begun, first, count):
    blocks, *own = retarded.shape[1:]
    rest = blocks - begun.shape[1]
    return pl.pallas_call(
        functools.partial(lesser_rest_kernel, first),
        out_shape=[kept((count, rest, *own)), kept((count, blocks, *own))],
        in_specs=[HBM, HBM, VMEM],
        out_specs=[VMEM, VMEM],
        scratch_shapes=lesser_scratch(count, rest, own),
        cost_estimate=lesser_cost(count, rest, own[-1]),
        compiler_params=PARAMS,
        name="lesser_rest",
    )(retarded, sigma_in, *in_vmem([begun]))


def lesser_couple_kernel(first, place_ref, neighbors_ref, coupling_ref, *refs):
    retarded_ref, sigma_ref, *out_refs, bent_ref, made, green, sigma, sems = refs
    blocks = retarded_ref.shape[1]
    count = out_refs[0].shape[0]
    loads = start_loads(
        first, count, range(blocks), retarded_ref, sigma_ref, green, sigma, sems
    )
    for start in range(0, len(loads), GROUP):
        group = range(start, min(start + GROUP, len(loads)))
        for i, both in lesser_items(loads, green, sigma, group):
            made[i % GROUP] = both
        for i in group:
            bend(coupling_ref, made[i % GROUP], bent_ref, i % blocks)
            if i % blocks == blocks - 1:
                unbend(place_ref, neighbors_ref, coupling_ref, bent_ref, out_refs, i // blocks)


def lesser_couple(place, neighbors, coupling, retarded, sigma_in, first, count, atoms):
    blocks, *own = retarded.shape[1:]
    directions, size, _ = coupling.shape
    return pl.pallas_call(
        functools.partial(lesser_couple_kernel, first),
        out_shape=[kept((count, blocks // atoms, *own))] * atoms,
        in_specs=[SMEM, SMEM, VMEM, HBM, HBM],
        out_specs=[VMEM] * atoms,
        scratch_shapes=[
            pltpu.VMEM((blocks, directions, *own), jnp.bfloat16),
            pltpu.VMEM((GROUP, size, own[0] * size), jnp.bfloat16),
        ]
        + lesser_scratch(count, blocks, own),
        cost_estimate=pl.CostEstimate(
            flops=count * blocks * (16 + directions * 8) * size**3,
            bytes_accessed=count * blocks * 12 * size**2,
            transcendentals=0,
        ),
        compiler_params=PARAMS,
        name="lesser_couple",
    )(place, neighbors, coupling, retarded, sigma_in)


def sum_couple_kernel(
    widths, place_ref, odd_ref, bit_shifts_ref, occupation_ref, neighbors_ref, coupling_ref, *refs
):
    taken = sum(widths)
    arrived, weights_ref, out_refs = list(refs[:taken]), refs[taken], refs[taken + 1 : -1]
    bent_ref = refs[-1]
    terms = [[arrived.pop(0) for _ in range(width)] for width in widths]
    weights = weights_of(len(terms), odd_ref, bit_shifts_ref, occupation_ref)
    for at, weight in enumerate(weights):
        weights_ref[at] = jnp.full(weights_ref.shape[1:], weight, jnp.float32)
    cuts = [piece.shape[1] for piece in max(terms, key=len)]
    for piece, span in enumerate(cuts):
        before = sum(cuts[:piece])

        def one(at, piece=piece, before=before):
            parts = []
            for part in range(2):
                total = None
                for weight, term in zip(weights, terms):
                    block = at if len(term) > 1 else before + at
                    value = term[piece % len(term)][0, block, part].astype(jnp.float32)
                    total = weight * value if total is None else total + weight * value
                parts.append(total.astype(jnp.bfloat16))
            bend(coupling_ref, jnp.concatenate(parts, axis=1), bent_ref, before + at)

        over_blocks(span, one)
    unbend(place_ref, neighbors_ref, coupling_ref, bent_ref, out_refs, 0)


def sum_couple(scalars, coupling, terms, atoms):
    count, blocks, *own = min(terms, key=len)[0].shape
    directions = coupling.shape[0]
    arrays = [array for term in terms for array in term]
    return pl.pallas_call(
        functools.partial(sum_couple_kernel, [len(term) for term in terms]),
        out_shape=[pltpu.VMEM((len(terms), 8, own[-1]), jnp.float32)]
        + [jax.ShapeDtypeStruct((count, blocks // atoms, *own), jnp.bfloat16)] * atoms,
        grid=(count,),
        in_specs=[SMEM] * len(scalars)
        + [VMEM]
        + [pl.BlockSpec((1, *array.shape[1:]), lambda e: (e, 0, 0, 0, 0)) for array in arrays],
        out_specs=[VMEM]
        + [
            pl.BlockSpec((1, blocks // atoms, *own), lambda e: (e, 0, 0, 0, 0))
            for _ in range(atoms)
        ],
        scratch_shapes=[pltpu.VMEM((blocks, directions, *own), jnp.bfloat16)],
        cost_estimate=pl.CostEstimate(
            flops=count * blocks * directions * 8 * own[-1] ** 3,
            bytes_accessed=count * blocks * 12 * own[-1] ** 2,
            transcendentals=0,
        ),
        compiler_params=PARAMS,
        name="sum_couple",
    )(*scalars, coupling, *arrays)


def weights_of(bits, odd_ref, bit_shifts_ref, occupation_ref):
    weights = []
    for bit in range(bits):
        weight = jnp.float32(0)
        for mode in range(bit_shifts_ref.shape[0]):
            weight += jnp.where(bit_shifts_ref[mode] == bit, occupation_ref[mode], 0.0)
        weights.append(weight)
    if bits > 1:
        odd = odd_ref[0] == 1
        low, high = weights[-2:]
        weights[-2:] = [jnp.where(odd, low, high), jnp.where(odd, high, low)]
    return weights


def gather_kernel(distances, place_ref, *refs):
    pieces, out_ref, sems = refs[:distances], refs[distances], refs[distances + 1]
    count = pieces[0].shape[0]
    per = out_ref.shape[0] // distances
    copies = []
    for distance, piece in enumerate(pieces):
        rows = pl.ds((place_ref[0] ^ distance) * per, count)
        copies.append(pltpu.make_async_copy(piece, out_ref.at[rows], sems.at[distance]))
        copies[-1].start()
    for copy in copies:
        copy.wait()


def place_first(place, pieces, energies):
    own = pieces[0].shape[1:]
    return pl.pallas_call(
        functools.partial(gather_kernel, len(pieces)),
        out_shape=jax.ShapeDtypeStruct((len(pieces) * energies, *own), jnp.bfloat16),
        in_specs=[SMEM] + [VMEM] * len(pieces),
        out_specs=ANY,
        scratch_shapes=[pltpu.SemaphoreType.DMA((len(pieces),))],
        compiler_params=PARAMS,
        name="place_first",
    )(place, *in_vmem(pieces))


def weighted_kernel(terms, energies, first, near, weights_ref, *refs):
    arrived, (last_ref, _, out_ref, result, sems) = refs[: terms - 1], refs[terms - 1 :]
    weights = [weights_ref[at, :1] for at in range(terms)]
    place = lax.axis_index("atom")
    distances, count = result.shape[:2]
    stores = []
    for d in range(distances):
        for e in range(count):
            total = weights[-1] * last_ref[d, e].astype(jnp.float32)
            for weight, term in zip(weights, arrived):
                total += weight * term[near + d, e].astype(jnp.float32)
            result[d, e] = total.astype(jnp.bfloat16)
            row = (place ^ (near + d)) * energies + first + e
            store = pltpu.make_async_copy(result.at[d, e], out_ref.at[row], sems.at[d, e])
            store.start()
            stores.append(store)
    for store in stores:
        store.wait()


def place_sum(weights, arrived, last, out, energies, first, near):
    terms = len(arrived) + 1
    return pl.pallas_call(
        functools.partial(weighted_kernel, terms, energies, first, near),
        out_shape=jax.ShapeDtypeStruct(out.shape, out.dtype),
        in_specs=[VMEM] * (terms + 1) + [ANY],
        out_specs=ANY,
        scratch_shapes=[
            pltpu.VMEM(last.shape, jnp.bfloat16),
            pltpu.SemaphoreType.DMA(last.shape[:2]),
        ],
        input_output_aliases={terms + 1: 0},
        compiler_params=PARAMS,
        cost_estimate=pl.CostEstimate(
            flops=2 * terms * last.size, bytes_accessed=2 * (terms + 1) * last.size, transcendentals=0
        ),
        name="place_sum",
    )(*in_vmem([weights]), *in_vmem([*arrived, last]), out)


def stack_kernel(near, *refs):
    *pieces, whole_ref, near_ref, far_ref, sems = refs
    copies = []
    for distance, piece in enumerate(pieces):
        part = near_ref.at[distance] if distance < near else far_ref.at[distance - near]
        for at, target in enumerate((whole_ref.at[distance], part)):
            copies.append(pltpu.make_async_copy(piece, target, sems.at[at, distance]))
            copies[-1].start()
    for copy in copies:
        copy.wait()


def stack(pieces, near):
    own, count = pieces[0].shape, len(pieces)
    return pl.pallas_call(
        functools.partial(stack_kernel, near),
        out_shape=[
            jax.ShapeDtypeStruct((size, *own), jnp.bfloat16) for size in (count, near, count - near)
        ],
        in_specs=[VMEM] * count,
        out_specs=[ANY] * 3,
        scratch_shapes=[pltpu.SemaphoreType.DMA((2, count))],
        compiler_params=PARAMS,
        name="stack",
    )(*in_vmem(pieces))


def term_masks(count):
    bits = count.bit_length() - 1
    masks = [(2**bit, 2**bit) for bit in range(bits)]
    if bits > 1:
        low, high = 2 ** (bits - 2), 2 ** (bits - 1)
        masks[-2:] = [(low, high), (high, low)]
    return masks


def oddness(window, count):
    bits = count.bit_length() - 1
    return (window >> (bits - 1) ^ window >> (bits - 2)) & 1 if bits > 1 else window & 0


def exchange(value, term):
    count = lax.axis_size("win")
    masks = term_masks(count)[term]
    pairs = [(source, source ^ masks[oddness(source, count)]) for source in range(count)]
    return lax.ppermute(value, "win", pairs)


def on_device(retarded, sigma_in, bit_shifts, occupation, neighbors, coupling):
    energies, blocks = retarded.shape[:2]
    atoms = lax.axis_size("atom")
    windows = lax.axis_size("win")
    terms = len(term_masks(windows))
    half = energies // 2
    rest = energies - half
    cut = blocks * 3 // 8
    place = lax.axis_index("atom").astype(jnp.int32).reshape(1)
    odd = oddness(lax.axis_index("win"), windows).astype(jnp.int32).reshape(1)
    retarded, sigma_in = [
        pltpu.with_memory_space_constraint(array, pltpu.HBM) for array in (retarded, sigma_in)
    ]
    table = neighbors.T
    begun = lesser_begin(retarded, sigma_in, 0, half, cut)
    arrived_begun = exchange(begun, terms - 2)
    ended, lesser_a = lesser_rest(retarded, sigma_in, begun, 0, half)
    arrived_ended = exchange(ended, terms - 2)
    arrived_a = {}
    for term in reversed(range(terms)):
        if term != terms - 2:
            arrived_a[term] = [exchange(lesser_a, term)]
    arrived_a[terms - 2] = [arrived_begun, arrived_ended]

    coupled_b = lesser_couple(
        place, table, coupling, retarded, sigma_in, half, rest, atoms
    )
    exchanged_b = [coupled_b[0]]
    for distance in range(1, atoms):
        exchanged_b.append(flip(coupled_b[distance], "atom", distance))
    near = atoms - max(atoms // NEARS, 1)
    whole_b, near_b, far_b = stack(exchanged_b, near)
    arrived_b = []
    for term in range(terms - 1):
        arrived_b.append(exchange(whole_b, term))
    arrived_near = exchange(near_b, terms - 1)
    arrived_far = exchange(far_b, terms - 1)

    weights, *coupled_a = sum_couple(
        (place, odd, bit_shifts, occupation, table),
        coupling,
        [arrived_a[term] for term in range(terms)],
        atoms,
    )
    exchanged_a = [coupled_a[0]]
    for distance in range(1, atoms):
        exchanged_a.append(flip(coupled_a[distance], "atom", distance))
    out = place_first(place, exchanged_a, energies)
    out = place_sum(weights, arrived_b, arrived_near, out, energies, half, 0)
    return place_sum(weights, arrived_b, arrived_far, out, energies, half, near)


def solution(mesh):
    return jax.shard_map(
        on_device,
        mesh=mesh,
        in_specs=(
            P(("win", "atom"), None, None, None, None),
            P(("win", "atom"), None, None, None, None),
            P(),
            P(),
            P(),
            P(),
        ),
        out_specs=P("win", "atom", None, None, None),
        check_vma=False,
    )
```
